512 devices in a mesh: tok: 64 (over y_lo, z, core), head: 8 (over x, y_hi).
Axes of the slice: x: 4, y: 4 (y_hi: 2, y_lo: 2; y = y_hi * 2 + y_lo), z: 16, core: 2. Of those that a mesh axis runs over, the one named last changes fastest.
Arguments:
- query_rows: bfloat16 [16384, 40, 128], P('tok', 'head'), as said below
- key_rows: bfloat16 [16384, 40, 128], P('tok', 'head'), as said below
- value_rows: bfloat16 [16384, 40, 128], P('tok', 'head'), may hold values from -6 to 6
- query_gain: float32 [40, 128], P('head'), may hold values from 1.5 to 4
- key_gain: float32 [40, 128], P('head'), may hold values from 0.25 to 1.75
- rate_in: float32 [40, 16384], P('head', 'tok'), may hold values from 0.05 to 0.5
- rate_out: float32 [40, 16384], P('head', 'tok'), may hold values from 0.0002 to 0.002
- fast_in: bfloat16 [40, 128, 512], P('head'), may hold values from -6 to 6
- fast_out: bfloat16 [40, 256, 128], P('head'), may hold values from -0.375 to 0.375
- half_window: int32 [40], P('head'), may hold values from 128 to 1024, as said below
- boundaries: int32 [3], replicated, may hold values from 2049 to 16383, as said below
Outputs:
- layer_out: bfloat16 [16384, 40, 128], P('tok', 'head')
The draws below stay inside these ranges and needn't reach their ends.
Inputs may be any that keep to these rules, and one draw needn't show every extreme that they name: `half_window`: no head sees more than 1024 tokens on either side; some head has exactly 1024 and some head exactly 128. `boundaries`: non-decreasing; the first is 2049 and the last 16383. `query_rows`: entries within -400 and 400. `key_rows`: entries within -400 and 400.
All inputs are finite; a program needn't handle non-finite values.
Results may differ from the reference program's by a relative error of at most 0.02.
Values may be sent and summed in bfloat16 or wider, within the bound.
A program may use at most 64 MiB of HBM per device.

```python
import math
import jax
import jax.numpy as jnp
from jax import lax

HEADS = 40
HEAD_DIM = 128
FAST_HID = 256
HALF = 1024
BOUNDS = 3
TOKENS = 16384


def pair_rows(key):
    base_key = jax.random.fold_in(key, 7)
    key_draw, query_draw = jax.random.split(base_key, 2)
    full_shape = (TOKENS, HEADS, HEAD_DIM)
    key_part = jnp.clip(jax.random.normal(key_draw, full_shape, jnp.float32), -6.0, 6.0)
    query_part = jnp.clip(jax.random.normal(query_draw, full_shape, jnp.float32), -6.0, 6.0)
    head_ramp = jnp.sqrt(1.0 + 2.0 * jnp.arange(HEADS, dtype=jnp.float32) / (HEADS - 1))
    key_part = key_part * head_ramp[None, :, None]
    query_part = query_part * head_ramp[None, :, None]
    return (query_part, key_part)


def draw_query_rows(key, part):
    return pair_rows(key)[0].astype(jnp.bfloat16)


def draw_key_rows(key, part):
    return pair_rows(key)[1].astype(jnp.bfloat16)


def draw_half_window(key, part):
    widths = jax.random.randint(jax.random.fold_in(key, 21), (HEADS,), HALF // 8, HALF + 1)
    widest = jax.random.randint(jax.random.fold_in(key, 22), (), 0, HEADS)
    offset = jax.random.randint(jax.random.fold_in(key, 23), (), 1, HEADS)
    narrowest = (widest + offset) % HEADS
    head_ids = jnp.arange(HEADS)
    widths = jnp.where(head_ids == narrowest, HALF // 8, widths)
    return jnp.where(head_ids == widest, HALF, widths).astype(jnp.int32)


def draw_boundaries(key, part):
    starts = jax.random.randint(jax.random.fold_in(key, 31), (BOUNDS,), 2 * HALF + 1, TOKENS)
    starts = jnp.sort(starts)
    slot_ids = jnp.arange(BOUNDS, dtype=jnp.int32)
    starts = jnp.where(slot_ids == 0, 2 * HALF + 1, starts)
    starts = jnp.where(slot_ids == BOUNDS - 1, TOKENS - 1, starts)
    return starts.astype(jnp.int32)


def steps_of(stream_key, dims, cuts, low, top_value):
    gain = 1.0
    for dim, blocks in cuts:
        steps = jax.random.uniform(jax.random.fold_in(jax.random.fold_in(stream_key, 6), dim), (blocks,), jnp.float32, low / len(cuts), top_value / len(cuts))
        gain = gain * jnp.repeat(jnp.exp(steps), dims[dim] // blocks).reshape((-1,) + (1,) * (len(dims) - 1 - dim))
    return gain


def gaussian(rng, dims, deviation, reach, cuts=(), kind=jnp.bfloat16):
    level = steps_of(rng, dims, cuts, -0.22, 0.18) if cuts else 1.0
    values = jax.random.normal(rng, dims, jnp.float32) * deviation * level
    return jnp.minimum(jnp.maximum(values, -reach), reach).astype(kind)


def setup_inputs(seed: int = 0) -> dict:
    key_list = jax.random.split(jax.random.key(seed), 12)
    query_rows = draw_query_rows(jax.random.fold_in(key_list[11], 71), 0)
    key_rows = draw_key_rows(jax.random.fold_in(key_list[11], 71), 0)
    value_rows = gaussian(key_list[2], (TOKENS, HEADS, HEAD_DIM), 1.0, 6.0, ((0, 64), (1, 8)))
    query_gain = jnp.clip(jnp.exp(math.log(4.0) - 0.98082925 * jax.random.uniform(key_list[3], (HEADS, HEAD_DIM), jnp.float32) ** steps_of(key_list[3], (HEADS, HEAD_DIM), ((0, 8),), -0.2, 0.2)), 1.5, 4.0)
    key_gain = jnp.clip(1.0 + 0.15 * jax.random.normal(key_list[4], (HEADS, HEAD_DIM), jnp.float32), 0.25, 1.75)
    rate_in = jnp.clip(jnp.exp(math.log(0.5) - 2.3025851 * jax.random.uniform(key_list[5], (HEADS, TOKENS), jnp.float32) ** steps_of(key_list[5], (HEADS, TOKENS), ((0, 8), (1, 64)), -0.2, 0.2)), 0.05, 0.5)
    rate_out = jnp.clip(jnp.exp(math.log(0.002) - 2.3025852 * jax.random.uniform(key_list[6], (HEADS, TOKENS), jnp.float32) ** steps_of(key_list[6], (HEADS, TOKENS), ((0, 8), (1, 64)), -0.2, 0.2)), 0.0002, 0.002)
    fast_in = gaussian(key_list[7], (HEADS, HEAD_DIM, 2 * FAST_HID), 1.0, 6.0, ((0, 8),))
    fast_out = gaussian(key_list[8], (HEADS, FAST_HID, HEAD_DIM), FAST_HID ** -0.5, 0.375, ((0, 8),))
    half_window = draw_half_window(jax.random.fold_in(key_list[11], 71), 0)
    boundaries = draw_boundaries(jax.random.fold_in(key_list[11], 71), 0)
    return {"query_rows": query_rows, "key_rows": key_rows, "value_rows": value_rows, "query_gain": query_gain, "key_gain": key_gain, "rate_in": rate_in, "rate_out": rate_out, "fast_in": fast_in, "fast_out": fast_out, "half_window": half_window, "boundaries": boundaries}


epsilon = 1e-06

def clip_of(places, boundaries):
    return lax.optimization_barrier(jnp.sum((places[:, None] >= boundaries[None, :]).astype(jnp.int32), axis=1))

def rms_rows(matrix, gain_row):
    as_float = matrix.astype(jnp.float32)
    mean_sq = lax.optimization_barrier(jnp.mean(as_float * as_float, axis=(1, 2), keepdims=True))
    return (as_float * lax.rsqrt(mean_sq + epsilon) * gain_row[None].astype(jnp.float32)).astype(jnp.bfloat16)

def unit_rows(matrix):
    as_float = matrix.astype(jnp.float32)
    return (as_float * lax.rsqrt(lax.optimization_barrier(jnp.sum(as_float * as_float, axis=-1, keepdims=True)) + epsilon)).astype(jnp.bfloat16)

def attend_head(query_head, key_head, value_head, half_reach, boundaries):
    block_rows = math.gcd(TOKENS, 512)
    zero_rows = jnp.zeros((HALF, HEAD_DIM), key_head.dtype)
    key_pad = jnp.concatenate([zero_rows, key_head, zero_rows], axis=0)
    value_pad = jnp.concatenate([zero_rows, value_head, zero_rows], axis=0)
    key_span = block_rows + 2 * HALF
    scaling = 1.0 / math.sqrt(HEAD_DIM)

    def one_block(block_index):
        first_row = (block_index * block_rows).astype(jnp.int32)
        query_block = lax.dynamic_slice_in_dim(query_head, first_row, block_rows, 0)
        key_block = lax.dynamic_slice_in_dim(key_pad, first_row, key_span, 0)
        value_block = lax.dynamic_slice_in_dim(value_pad, first_row, key_span, 0)
        scores = jnp.dot(query_block, key_block.T, preferred_element_type=jnp.float32) * scaling
        query_places = first_row + jnp.arange(block_rows, dtype=jnp.int32)
        key_places = first_row - HALF + jnp.arange(key_span, dtype=jnp.int32)
        inside = (key_places >= 0) & (key_places < TOKENS)
        same_clip = clip_of(query_places, boundaries)[:, None] == clip_of(key_places, boundaries)[None, :]
        allowed = (jnp.abs(query_places[:, None] - key_places[None, :]) <= half_reach) & inside[None, :] & same_clip
        masked = jnp.where(allowed, scores, -jnp.inf)
        row_max = lax.optimization_barrier(jnp.max(masked, axis=1, keepdims=True))
        weights = jnp.exp(masked - row_max)
        denominator = lax.optimization_barrier(jnp.sum(weights, axis=1, keepdims=True))
        return jnp.dot(weights.astype(jnp.bfloat16), value_block, preferred_element_type=jnp.float32) / denominator
    blocks = lax.map(one_block, jnp.arange(TOKENS // block_rows, dtype=jnp.int32))
    return blocks.reshape(TOKENS, HEAD_DIM)

def renormed(initial, gradient):
    base = initial.astype(jnp.float32)
    updated = base - gradient
    base_norm = jnp.sqrt(lax.optimization_barrier(jnp.sum(base * base, axis=0)))
    factor = base_norm / jnp.sqrt(lax.optimization_barrier(jnp.sum(updated * updated, axis=0)) + epsilon)
    return (updated * factor[None, :]).astype(jnp.bfloat16)

def fast_head(query_unit, key_unit, value_head, rate_in_head, rate_out_head, fast_in_head, fast_out_head):
    pre_keys = jnp.dot(key_unit, fast_in_head, preferred_element_type=jnp.float32)
    gate_part = pre_keys[:, :FAST_HID]
    lin_part = pre_keys[:, FAST_HID:]
    sigmoid_gate = jax.nn.sigmoid(gate_part)
    swish_gate = gate_part * sigmoid_gate
    hidden = (swish_gate * lin_part).astype(jnp.bfloat16)
    value_float = value_head.astype(jnp.float32)
    push_out = (-rate_out_head[:, None] * value_float).astype(jnp.bfloat16)
    push_in = (-rate_in_head[:, None] * value_float).astype(jnp.bfloat16)
    grad_out = jnp.dot(hidden.T, push_out, preferred_element_type=jnp.float32)
    hidden_grad = jnp.dot(push_in, fast_out_head.T, preferred_element_type=jnp.float32)
    d_gate = hidden_grad * lin_part * sigmoid_gate * (1.0 + gate_part * (1.0 - sigmoid_gate))
    d_lin = hidden_grad * swish_gate
    d_pre = jnp.concatenate([d_gate, d_lin], axis=1).astype(jnp.bfloat16)
    grad_in = jnp.dot(key_unit.T, d_pre, preferred_element_type=jnp.float32)
    new_in = renormed(fast_in_head, grad_in)
    new_out = renormed(fast_out_head, grad_out)
    pre_query = jnp.dot(query_unit, new_in, preferred_element_type=jnp.float32)
    query_hidden = (jax.nn.silu(pre_query[:, :FAST_HID]) * pre_query[:, FAST_HID:]).astype(jnp.bfloat16)
    return jnp.dot(query_hidden, new_out, preferred_element_type=jnp.float32)

def reference(query_rows, key_rows, value_rows, query_gain, key_gain, rate_in, rate_out, fast_in, fast_out, half_window, boundaries):
    q_normed = rms_rows(query_rows, query_gain)
    k_normed = rms_rows(key_rows, key_gain)
    query_unit = unit_rows(q_normed)
    key_unit = unit_rows(k_normed)

    def per_head(head_items):
        q_head, k_head, v_head, qu_head, ku_head, rin_head, rout_head, fin_head, fout_head, half_reach = head_items
        attended = attend_head(q_head, k_head, v_head, half_reach, boundaries)
        fast_result = fast_head(qu_head, ku_head, v_head, rin_head, rout_head, fin_head, fout_head)
        return (attended + fast_result).astype(jnp.bfloat16)
    heads_first = (jnp.transpose(q_normed, (1, 0, 2)), jnp.transpose(k_normed, (1, 0, 2)), jnp.transpose(value_rows, (1, 0, 2)), jnp.transpose(query_unit, (1, 0, 2)), jnp.transpose(key_unit, (1, 0, 2)), rate_in, rate_out, fast_in, fast_out, half_window)
    result = lax.map(per_head, heads_first)
    return jnp.transpose(result, (1, 0, 2))
```

```python
import math

import jax
import jax.numpy as jnp
from jax import lax
from jax.experimental import pallas as pl
from jax.experimental.pallas import tpu as pltpu
from jax.sharding import PartitionSpec as P

epsilon = 1e-06
MESH = pl.DeviceIdType.MESH
NEG = -1e30
GRAD_ROWS = 4096


def rows_to_columns(row, lanes):
    return jnp.transpose(jnp.broadcast_to(row, (lanes, row.shape[1])))


def silu_parts(gate):
    sigmoid = 1.0 / (1.0 + jnp.exp(-gate))
    return sigmoid, gate * sigmoid


def dot(a, b, dims=((1,), (0,))):
    return lax.dot_general(a, b, (dims, ((), ())), preferred_element_type=jnp.float32)


def kernel(
    heads_all,
    n_tok,
    n_head,
    q_ref,
    k_ref,
    v_ref,
    qg_ref,
    kg_ref,
    ri_ref,
    ro_ref,
    fi_ref,
    fo_ref,
    hw_ref,
    bd_ref,
    out_ref,
    kh,
    vh,
    ss_loc,
    ss_all,
    tot_all,
    qt,
    qu,
    m_ref,
    l_ref,
    acc,
    grad,
    rc,
    s1,
    ry,
    qb,
    rz,
    wsum,
    fast,
    ss_send,
    ss_recv,
    tot_send,
    tot_recv,
    hk_send,
    hk_recv,
    hv_send,
    hv_recv,
    rc_sem,
    ry_sem,
    rz_send,
    rz_recv,
    az_send,
    az_recv,
    ay_sem,
    ac_sem,
):
    local_heads, rows, dim = k_ref.shape
    hid = fo_ref.shape[1]
    total_tokens = rows * n_tok
    chips = n_tok // 2
    nz = chips // 2
    part = GRAD_ROWS // (4 * nz)
    t = lax.axis_index("tok")
    me_head = lax.axis_index("head")
    core = t % 2
    chip = t // 2
    z = chip % nz
    yl = chip // nz
    partner = t + 1 - 2 * core
    y_peer = (1 - yl) * (2 * nz) + z * 2 + core

    def z_peer(i):
        return yl * (2 * nz) + ((z + i) % nz) * 2 + core

    def tok_ring(off):
        return (t + off + n_tok) % n_tok

    def at_tok(dev):
        return (dev, me_head)

    barrier = pltpu.get_barrier_semaphore()

    def greet(dev):
        pl.semaphore_signal(barrier, inc=1, device_id=dev, device_id_type=MESH)

    for off in (1, 2, 3, 4):
        greet(at_tok(tok_ring(off)))
        greet(at_tok(tok_ring(-off)))
    for i in range(1, n_head):
        greet((t, (me_head + i) % n_head))
    for i in range(1, nz):
        greet(at_tok(z_peer(i)))
    greet(at_tok(y_peer))
    pl.semaphore_wait(barrier, 8 + (n_head - 1) + (nz - 1) + 1)

    def remote(src, dst, send, recv, dev):
        return pltpu.make_async_remote_copy(
            src_ref=src,
            dst_ref=dst,
            send_sem=send,
            recv_sem=recv,
            device_id=dev,
            device_id_type=MESH,
        )

    def halo(ref, buf, send, recv, slot, dev):
        return remote(ref, buf.at[slot], send.at[slot], recv.at[slot], at_tok(dev))

    near = ((1, tok_ring(2)), (2, tok_ring(-2)))
    far = ((0, tok_ring(4)), (3, tok_ring(-4)))
    k_copy = {}
    v_copy = {}
    for slot, dev in near + far:
        k_copy[slot] = halo(k_ref, kh, hk_send, hk_recv, slot, dev)
        v_copy[slot] = halo(v_ref, vh, hv_send, hv_recv, slot, dev)
    far_src = 3 * (1 - core)
    for slot, src in ((4, 1), (6, 2), (7, far_src)):
        k_copy[slot] = halo(kh.at[src], kh, hk_send, hk_recv, slot, partner)
        v_copy[slot] = halo(vh.at[src], vh, hv_send, hv_recv, slot, partner)
    k_copy[5] = halo(k_ref, kh, hk_send, hk_recv, 5, partner)
    v_copy[5] = halo(v_ref, vh, hv_send, hv_recv, 5, partner)
    side = 1 - 2 * core
    slot_off = {0: -4, 1: -2, 2: 2, 3: 4, 4: side - 2, 5: side, 6: side + 2, 7: -3 * side}

    for slot, _ in near:
        k_copy[slot].start()
    k_copy[5].start()
    v_copy[5].start()

    k_sq = jnp.zeros((rows, dim), jnp.float32)
    q_sq = jnp.zeros((rows, dim), jnp.float32)
    for h in range(local_heads):
        kf = k_ref[h].astype(jnp.float32)
        qf = q_ref[h].astype(jnp.float32)
        k_sq = k_sq + kf * kf
        q_sq = q_sq + qf * qf
    k_row = jnp.sum(jnp.transpose(k_sq), axis=0, keepdims=True)
    q_row = jnp.sum(jnp.transpose(q_sq), axis=0, keepdims=True)
    sub = lax.broadcasted_iota(jnp.int32, (8, rows), 0)
    ss_loc[...] = jnp.where(
        sub == 0, jnp.broadcast_to(k_row, (8, rows)), jnp.broadcast_to(q_row, (8, rows))
    )

    def ss_copy(i):
        other = (me_head + i) % n_head
        return remote(
            ss_loc, ss_all.at[me_head], ss_send.at[other], ss_recv.at[me_head], (t, other)
        )

    def ss_arrival(i):
        other = (me_head + i) % n_head
        return remote(
            ss_loc, ss_all.at[other], ss_send.at[other], ss_recv.at[other], (t, other)
        )

    for i in range(1, n_head):
        ss_copy(i).start()
    total = ss_loc[...]
    for i in range(1, n_head):
        ss_arrival(i).wait_recv()
        total = total + ss_all[(me_head + i) % n_head]
    tot_all[4] = total

    def tot_copy(off):
        return remote(
            tot_all.at[4],
            tot_all.at[4 - off],
            tot_send.at[4 - off],
            tot_recv.at[4 - off],
            at_tok(tok_ring(off)),
        )

    offsets = (1, -1, 2, -2, 3, -3, 4, -4)
    for off in offsets:
        tot_copy(off).start()
    for slot, _ in near:
        v_copy[slot].start()

    inv_width = 1.0 / (heads_all * dim)

    def scale_of(sums_row):
        return rows_to_columns(lax.rsqrt(sums_row * inv_width + epsilon), dim)

    def normed(block, scale, gain):
        return (block.astype(jnp.float32) * scale * gain).astype(jnp.bfloat16)

    def unit(block):
        as_float = block.astype(jnp.float32)
        squares = jnp.sum(as_float * as_float, axis=1, keepdims=True)
        return (as_float * lax.rsqrt(squares + epsilon)).astype(jnp.bfloat16)

    k_scale = scale_of(total[0:1])
    q_scale = scale_of(total[1:2])

    pad_rows = GRAD_ROWS - local_heads * 6 * 128
    grad[pl.ds(GRAD_ROWS - pad_rows, pad_rows)] = jnp.zeros((pad_rows, dim), jnp.bfloat16)

    def grads(h, carry):
        key_unit = unit(normed(k_ref[h], k_scale, kg_ref[pl.ds(h, 1)]))
        pre = dot(key_unit, fi_ref[h])
        gate = pre[:, :hid]
        lin = pre[:, hid:]
        sigmoid, swish = silu_parts(gate)
        hidden = (swish * lin).astype(jnp.bfloat16)
        value = v_ref[h].astype(jnp.float32)
        push_out = (-rows_to_columns(ro_ref[pl.ds(h, 1)], dim) * value).astype(jnp.bfloat16)
        push_in = (-rows_to_columns(ri_ref[pl.ds(h, 1)], dim) * value).astype(jnp.bfloat16)
        grad_out = dot(hidden, push_out, ((0,), (0,)))
        hidden_grad = dot(push_in, fo_ref[h], ((1,), (1,)))
        d_gate = hidden_grad * lin * sigmoid * (1.0 + gate * (1.0 - sigmoid))
        d_lin = hidden_grad * swish
        first = h * 768
        for j, d_part in enumerate((d_gate, d_lin)):
            grad_in = dot(key_unit, d_part.astype(jnp.bfloat16), ((0,), (0,)))
            for half in range(2):
                start = pl.multiple_of(first + (2 * j + half) * 128, 128)
                grad[pl.ds(start, 128)] = grad_in[:, half * 128 : half * 128 + 128].astype(
                    jnp.bfloat16
                )
        start = pl.multiple_of(first + 512, 128)
        grad[pl.ds(start, 256)] = grad_out.astype(jnp.bfloat16)
        return carry

    lax.fori_loop(0, local_heads, grads, 0)

    half_rows = GRAD_ROWS // 2
    quarter = GRAD_ROWS // 4

    def half_at(which):
        return pl.multiple_of(which * half_rows, half_rows)

    rc_copy = remote(
        grad.at[pl.ds(half_at(1 - core), half_rows)],
        rc,
        rc_sem.at[0],
        rc_sem.at[1],
        at_tok(partner),
    )
    rc_copy.start()

    scaling = math.log2(math.e) / math.sqrt(dim)

    def queries(h, carry):
        raw = q_ref[h].astype(jnp.float32) * q_scale * qg_ref[pl.ds(h, 1)]
        qt[h] = jnp.transpose(raw * scaling).astype(jnp.bfloat16)
        qu[h] = unit(raw.astype(jnp.bfloat16))
        return carry

    lax.fori_loop(0, local_heads, queries, 0)

    positions = t * rows + lax.broadcasted_iota(jnp.int32, (1, rows), 1)
    clip_first = jnp.zeros((1, rows), jnp.int32)
    clip_last = jnp.full((1, rows), total_tokens - 1, jnp.int32)
    for b in range(bd_ref.shape[0]):
        edge = bd_ref[b]
        clip_first = jnp.where(positions >= edge, jnp.maximum(clip_first, edge), clip_first)
        clip_last = jnp.where(positions < edge, jnp.minimum(clip_last, edge - 1), clip_last)

    def absorb(keys, values, off, first=False):
        scale = k_scale if first else scale_of(tot_all[off + 4][0:1])
        places = (t + off) * rows + lax.broadcasted_iota(jnp.int32, (rows, rows), 0)

        def one(h, carry):
            window = hw_ref[h]
            low = jnp.maximum(positions - window, clip_first)
            high = jnp.minimum(positions + window, clip_last)
            block = normed(keys[h], scale, kg_ref[pl.ds(h, 1)])
            scores = dot(block, qt[h])
            scores = jnp.where((places >= low) & (places <= high), scores, NEG)
            best = jnp.max(scores, axis=0, keepdims=True)
            if not first:
                best_old = m_ref[pl.ds(h, 1)]
                best = jnp.maximum(best, best_old)
            weights = jnp.exp2(scores - best)
            denom = jnp.sum(weights, axis=0, keepdims=True)
            product = dot(values[h], weights.astype(jnp.bfloat16), ((0,), (0,)))
            if not first:
                shrink = jnp.exp2(best_old - best)
                denom = denom + l_ref[pl.ds(h, 1)] * shrink
                product = product + acc[h] * shrink
            m_ref[pl.ds(h, 1)] = best
            l_ref[pl.ds(h, 1)] = denom
            acc[h] = product
            return carry

        lax.fori_loop(0, local_heads, one, 0)

    def absorb_slot(slot):
        absorb(kh.at[slot], vh.at[slot], slot_off[slot])

    def arrived(slot):
        k_copy[slot].wait_recv()
        v_copy[slot].wait_recv()

    absorb(k_ref, v_ref, 0, first=True)

    rc_copy.wait_recv()

    def rows_of(ref, start, size):
        return ref[pl.ds(pl.multiple_of(start, size), size)].astype(jnp.float32)

    away = (1 - yl) * quarter
    for i in range(4):
        size = quarter // 4
        s1[pl.ds(i * size, size)] = (
            rows_of(grad, core * half_rows + away + i * size, size)
            + rows_of(rc, away + i * size, size)
        ).astype(jnp.bfloat16)
    ry_copy = remote(s1, ry, ry_sem.at[0], ry_sem.at[1], at_tok(y_peer))
    ry_copy.start()
    for off in offsets:
        tot_copy(off).wait_recv()
    arrived(5)
    absorb_slot(5)

    ry_copy.wait_recv()
    home = yl * quarter
    for i in range(4):
        size = quarter // 4
        qb[pl.ds(i * size, size)] = (
            rows_of(grad, core * half_rows + home + i * size, size)
            + rows_of(rc, home + i * size, size)
            + rows_of(ry, i * size, size)
        ).astype(jnp.bfloat16)

    def part_at(which):
        return pl.ds(pl.multiple_of(which * part, part), part)

    def rz_copy(i):
        other = (z + i) % nz
        return remote(
            qb.at[part_at(other)],
            rz.at[z],
            rz_send.at[other],
            rz_recv.at[z],
            at_tok(z_peer(i)),
        )

    def rz_arrival(i):
        other = (z + i) % nz
        return remote(
            qb.at[part_at(other)],
            rz.at[other],
            rz_send.at[other],
            rz_recv.at[other],
            at_tok(z_peer(i)),
        )

    for i in range(1, nz):
        rz_copy(i).start()
    for slot, _ in far:
        k_copy[slot].start()
        v_copy[slot].start()

    for slot in (1, 2):
        arrived(slot)
        k_copy[slot + (3 if slot == 1 else 4)].start()
        v_copy[slot + (3 if slot == 1 else 4)].start()
    absorb_slot(1)
    absorb_slot(2)

    summed = (
        rows_of(grad, core * half_rows + home + z * part, part)
        + rows_of(rc, home + z * part, part)
        + rows_of(ry, z * part, part)
    )
    for i in range(1, nz):
        rz_arrival(i).wait_recv()
        summed = summed + rz[(z + i) % nz].astype(jnp.float32)
    mine = core * half_rows + home

    def sum_at(which):
        return pl.ds(pl.multiple_of(mine + which * part, part), part)

    wsum[sum_at(z)] = summed.astype(jnp.bfloat16)

    def az_copy(i):
        other = (z + i) % nz
        return remote(
            wsum.at[sum_at(z)],
            wsum.at[sum_at(z)],
            az_send.at[other],
            az_recv.at[z],
            at_tok(z_peer(i)),
        )

    def az_arrival(i):
        other = (z + i) % nz
        return remote(
            wsum.at[sum_at(other)],
            wsum.at[sum_at(other)],
            az_send.at[other],
            az_recv.at[other],
            at_tok(z_peer(i)),
        )

    for i in range(1, nz):
        az_copy(i).start()

    arrived(4)
    absorb_slot(4)
    arrived(6)
    absorb_slot(6)

    for i in range(1, nz):
        az_arrival(i).wait_recv()
    quarter_at = pl.ds(pl.multiple_of(mine, quarter), quarter)
    other_quarter = pl.ds(pl.multiple_of(core * half_rows + away, quarter), quarter)
    ay_copy = remote(
        wsum.at[quarter_at], wsum.at[quarter_at], ay_sem.at[0], ay_sem.at[1], at_tok(y_peer)
    )
    ay_arrival = remote(
        wsum.at[other_quarter],
        wsum.at[other_quarter],
        ay_sem.at[0],
        ay_sem.at[1],
        at_tok(y_peer),
    )
    ay_copy.start()

    arrived(0)
    arrived(3)
    k_copy[7].start()
    v_copy[7].start()
    absorb_slot(0)

    ay_arrival.wait_recv()
    my_half = pl.ds(half_at(core), half_rows)
    other_half = pl.ds(half_at(1 - core), half_rows)
    ac_copy = remote(
        wsum.at[my_half], wsum.at[my_half], ac_sem.at[0], ac_sem.at[1], at_tok(partner)
    )
    ac_arrival = remote(
        wsum.at[other_half], wsum.at[other_half], ac_sem.at[0], ac_sem.at[1], at_tok(partner)
    )
    ac_copy.start()
    absorb_slot(3)
    arrived(7)
    absorb_slot(7)
    ac_arrival.wait_recv()

    def renewed(base, start, size):
        base = base.astype(jnp.float32)
        updated = base - wsum[pl.ds(pl.multiple_of(start, 128), size)].astype(jnp.float32)
        norm = jnp.sqrt(jnp.sum(base * base, axis=0, keepdims=True))
        squares = jnp.sum(updated * updated, axis=0, keepdims=True)
        return (updated * (norm / jnp.sqrt(squares + epsilon))).astype(jnp.bfloat16)

    def finish(h, carry):
        query_unit = qu[h]
        first = h * 768
        query_hidden = []
        for half in range(2):
            gate = dot(
                query_unit,
                renewed(fi_ref[h, :, half * 128 : half * 128 + 128], first + half * 128, 128),
            )
            lin = dot(
                query_unit,
                renewed(
                    fi_ref[h, :, hid + half * 128 : hid + half * 128 + 128],
                    first + 256 + half * 128,
                    128,
                ),
            )
            query_hidden.append((silu_parts(gate)[1] * lin).astype(jnp.bfloat16))
        new_out = renewed(fo_ref[h], first + 512, hid)
        result = dot(jnp.concatenate(query_hidden, axis=1), new_out)
        attended = jnp.transpose(acc[h] / l_ref[pl.ds(h, 1)])
        out_ref[h] = (attended + result).astype(jnp.bfloat16)
        return carry

    lax.fori_loop(0, local_heads, finish, 0)

    for i in range(1, n_head):
        ss_copy(i).wait_send()
    for off in offsets:
        tot_copy(off).wait_send()
    for slot in range(8):
        k_copy[slot].wait_send()
        v_copy[slot].wait_send()
    rc_copy.wait_send()
    ry_copy.wait_send()
    for i in range(1, nz):
        rz_copy(i).wait_send()
        az_copy(i).wait_send()
    ay_copy.wait_send()
    ac_copy.wait_send()


def body(q, k, v, q_gain, k_gain, rate_in, rate_out, fast_in, fast_out, half_window, boundaries):
    rows, heads, dim = q.shape
    n_tok = lax.axis_size("tok")
    n_head = lax.axis_size("head")
    nz = n_tok // 4
    part = GRAD_ROWS // (4 * nz)
    bf16 = jnp.bfloat16
    f32 = jnp.float32
    vmem = pl.BlockSpec(memory_space=pltpu.VMEM)
    smem = pl.BlockSpec(memory_space=pltpu.SMEM)
    dma = pltpu.SemaphoreType.DMA

    def call(*refs):
        kernel(heads * n_head, n_tok, n_head, *refs)

    result = pl.pallas_call(
        call,
        out_shape=jax.ShapeDtypeStruct((heads, rows, dim), bf16),
        in_specs=[vmem] * 9 + [smem] * 2,
        out_specs=vmem,
        scratch_shapes=[
            pltpu.VMEM((8, heads, rows, dim), bf16),
            pltpu.VMEM((8, heads, rows, dim), bf16),
            pltpu.VMEM((8, rows), f32),
            pltpu.VMEM((n_head, 8, rows), f32),
            pltpu.VMEM((9, 8, rows), f32),
            pltpu.VMEM((heads, dim, rows), bf16),
            pltpu.VMEM((heads, rows, dim), bf16),
            pltpu.VMEM((8, rows), f32),
            pltpu.VMEM((8, rows), f32),
            pltpu.VMEM((heads, dim, rows), f32),
            pltpu.VMEM((GRAD_ROWS, dim), bf16),
            pltpu.VMEM((GRAD_ROWS // 2, dim), bf16),
            pltpu.VMEM((GRAD_ROWS // 4, dim), bf16),
            pltpu.VMEM((GRAD_ROWS // 4, dim), bf16),
            pltpu.VMEM((GRAD_ROWS // 4, dim), bf16),
            pltpu.VMEM((nz, part, dim), bf16),
            pltpu.VMEM((GRAD_ROWS, dim), bf16),
            pltpu.VMEM((8, 128), f32),
            dma((n_head,)),
            dma((n_head,)),
            dma((9,)),
            dma((9,)),
            dma((8,)),
            dma((8,)),
            dma((8,)),
            dma((8,)),
            dma((2,)),
            dma((2,)),
            dma((nz,)),
            dma((nz,)),
            dma((nz,)),
            dma((nz,)),
            dma((2,)),
            dma((2,)),
        ],
        compiler_params=pltpu.CompilerParams(
            collective_id=0, has_side_effects=True, vmem_limit_bytes=60 * 1024 * 1024
        ),
    )(
        jnp.transpose(q, (1, 0, 2)),
        jnp.transpose(k, (1, 0, 2)),
        jnp.transpose(v, (1, 0, 2)),
        q_gain,
        k_gain,
        rate_in,
        rate_out,
        fast_in,
        fast_out,
        half_window,
        boundaries,
    )
    return jnp.transpose(result, (1, 0, 2))


def solution(mesh):
    in_specs = (
        P("tok", "head", None),
        P("tok", "head", None),
        P("tok", "head", None),
        P("head", None),
        P("head", None),
        P("head", "tok"),
        P("head", "tok"),
        P("head", None, None),
        P("head", None, None),
        P("head"),
        P(),
    )
    out_specs = P("tok", "head", None)
    return jax.shard_map(body, mesh=mesh, in_specs=in_specs, out_specs=out_specs, check_vma=False)
```

```python
import math

import jax
import jax.numpy as jnp
from jax import lax
from jax.experimental import pallas as pl
from jax.experimental.pallas import tpu as pltpu
from jax.sharding import PartitionSpec as P

epsilon = 1e-06
MESH = pl.DeviceIdType.MESH
NEG = -1e30
HEAD_ROWS = 768
EIGHTH = 512


def far_first(n):
    return sorted(range(1, n), key=lambda i: (-min(i, n - i), i))


def rows_to_columns(row, lanes):
    return jnp.transpose(jnp.broadcast_to(row, (lanes, row.shape[1])))


def silu_parts(gate):
    sigmoid = 1.0 / (1.0 + jnp.exp(-gate))
    return sigmoid, gate * sigmoid


def dot(a, b, dims=((1,), (0,))):
    return lax.dot_general(a, b, (dims, ((), ())), preferred_element_type=jnp.float32)


def kernel(
    heads_all,
    n_tok,
    n_head,
    q_ref,
    k_ref,
    v_ref,
    qg_ref,
    kg_ref,
    ri_ref,
    ro_ref,
    fi_ref,
    fo_ref,
    hw_ref,
    bd_ref,
    out_ref,
    kh,
    vh,
    ss_loc,
    ss_all,
    tot_all,
    qt,
    qu,
    m_ref,
    l_ref,
    acc,
    pre_ref,
    push_ref,
    hg_ref,
    grad,
    rc,
    s1,
    ry,
    s2,
    rp,
    qb,
    rz,
    wsum,
    fast,
    ss_send,
    ss_recv,
    tot_send,
    tot_recv,
    hk_send,
    hk_recv,
    hv_send,
    hv_recv,
    rc_send,
    rc_recv,
    ry_send,
    ry_recv,
    rp_send,
    rp_recv,
    rz_send,
    rz_recv,
    az_send,
    az_recv,
    ap_send,
    ap_recv,
    ay_send,
    ay_recv,
    ac_send,
    ac_recv,
):
    local_heads, rows, dim = k_ref.shape
    hid = fo_ref.shape[1]
    total_tokens = rows * n_tok
    chips = n_tok // 2
    nz = chips // 2
    owners = nz // 2
    part = EIGHTH // owners
    t = lax.axis_index("tok")
    me_head = lax.axis_index("head")
    core = t % 2
    chip = t // 2
    z = chip % nz
    yl = chip // nz
    zp = z % 2
    zo = z // 2
    partner = t + 1 - 2 * core
    y_peer = (1 - yl) * (2 * nz) + z * 2 + core
    pair = yl * (2 * nz) + (z + 1 - 2 * zp) * 2 + core

    def z_peer(i):
        return yl * (2 * nz) + (((zo + i) % owners) * 2 + zp) * 2 + core

    def tok_ring(off):
        return (t + off + n_tok) % n_tok

    def at_tok(dev):
        return (dev, me_head)

    barrier = pltpu.get_barrier_semaphore()

    def greet(dev):
        pl.semaphore_signal(barrier, inc=1, device_id=dev, device_id_type=MESH)

    for i in far_first(owners):
        greet(at_tok(z_peer(i)))
    for i in range(1, n_head):
        greet((t, (me_head + i) % n_head))
    for off in (1, 2, 3, 4):
        greet(at_tok(tok_ring(off)))
        greet(at_tok(tok_ring(-off)))
    greet(at_tok(y_peer))
    greet(at_tok(pair))

    def remote(src, dst, send, recv, dev):
        return pltpu.make_async_remote_copy(
            src_ref=src,
            dst_ref=dst,
            send_sem=send,
            recv_sem=recv,
            device_id=dev,
            device_id_type=MESH,
        )

    def halo(ref, buf, send, recv, slot, dev):
        return remote(ref, buf.at[slot], send.at[slot], recv.at[slot], at_tok(dev))

    k_copy = {}
    v_copy = {}
    far_src = 3 * (1 - core)
    routes = (
        (1, None, tok_ring(2)),
        (2, None, tok_ring(-2)),
        (0, 1, tok_ring(2)),
        (3, 2, tok_ring(-2)),
        (4, 1, partner),
        (5, None, partner),
        (6, 2, partner),
        (7, far_src, partner),
    )
    for slot, src, dev in routes:
        k_src = k_ref if src is None else kh.at[src]
        v_src = v_ref if src is None else vh.at[src]
        k_copy[slot] = halo(k_src, kh, hk_send, hk_recv, slot, dev)
        v_copy[slot] = halo(v_src, vh, hv_send, hv_recv, slot, dev)
    side = 1 - 2 * core
    slot_off = {0: -4, 1: -2, 2: 2, 3: 4, 4: side - 2, 5: side, 6: side + 2, 7: -3 * side}

    k_sq = jnp.zeros((rows, dim), jnp.float32)
    q_sq = jnp.zeros((rows, dim), jnp.float32)
    for h in range(local_heads):
        kf = k_ref[h].astype(jnp.float32)
        qf = q_ref[h].astype(jnp.float32)
        k_sq = k_sq + kf * kf
        q_sq = q_sq + qf * qf
    k_row = jnp.sum(jnp.transpose(k_sq), axis=0, keepdims=True)
    q_row = jnp.sum(jnp.transpose(q_sq), axis=0, keepdims=True)
    sub = lax.broadcasted_iota(jnp.int32, (8, rows), 0)
    ss_loc[...] = jnp.where(
        sub == 0, jnp.broadcast_to(k_row, (8, rows)), jnp.broadcast_to(q_row, (8, rows))
    )

    pl.semaphore_wait(barrier, (owners - 1) + (n_head - 1) + 8 + 2)

    def ss_copy(i):
        other = (me_head + i) % n_head
        return remote(
            ss_loc, ss_all.at[me_head], ss_send.at[other], ss_recv.at[me_head], (t, other)
        )

    def ss_arrival(i):
        other = (me_head + i) % n_head
        return remote(
            ss_loc, ss_all.at[other], ss_send.at[other], ss_recv.at[other], (t, other)
        )

    for i in range(1, n_head):
        ss_copy(i).start()
    for slot in (1, 2, 5):
        k_copy[slot].start()

    def early(h, carry):
        key_gained = k_ref[h].astype(jnp.float32) * kg_ref[pl.ds(h, 1)]
        pre_ref[h] = dot(key_gained.astype(jnp.bfloat16), fi_ref[h])
        value = v_ref[h].astype(jnp.float32)
        push_ref[h] = (-rows_to_columns(ro_ref[pl.ds(h, 1)], dim) * value).astype(jnp.bfloat16)
        push_in = (-rows_to_columns(ri_ref[pl.ds(h, 1)], dim) * value).astype(jnp.bfloat16)
        hg_ref[h] = dot(push_in, fo_ref[h], ((1,), (1,)))
        return carry

    lax.fori_loop(0, local_heads, early, 0)
    for i in range(1, n_head):
        ss_arrival(i).wait_recv()
    total = ss_loc[...]
    for i in range(1, n_head):
        total = total + ss_all[(me_head + i) % n_head]
    tot_all[4] = total

    def tot_copy(off):
        return remote(
            tot_all.at[4],
            tot_all.at[4 - off],
            tot_send.at[4 - off],
            tot_recv.at[4 - off],
            at_tok(tok_ring(off)),
        )

    offsets = (1, -1, 2, -2, 3, -3, 4, -4)
    for off in offsets:
        tot_copy(off).start()
    for slot in (1, 2, 5):
        v_copy[slot].start()

    inv_width = 1.0 / (heads_all * dim)

    def scale_of(sums_row):
        return rows_to_columns(lax.rsqrt(sums_row * inv_width + epsilon), dim)

    def normed(block, scale, gain):
        return (block.astype(jnp.float32) * scale * gain).astype(jnp.bfloat16)

    def unit(block):
        as_float = block.astype(jnp.float32)
        squares = jnp.sum(as_float * as_float, axis=1, keepdims=True)
        return (as_float * lax.rsqrt(squares + epsilon)).astype(jnp.bfloat16)

    k_scale = scale_of(total[0:1])
    q_scale = scale_of(total[1:2])

    def rc_copy(h):
        return remote(
            grad.at[h, pl.ds(pl.multiple_of((1 - core) * 384, 384), 384)],
            rc.at[h],
            rc_send.at[h],
            rc_recv.at[h],
            at_tok(partner),
        )

    def grads(h, carry):
        raw = k_ref[h].astype(jnp.float32) * kg_ref[pl.ds(h, 1)]
        squares = jnp.sum(raw * raw, axis=1, keepdims=True)
        factor = k_scale * lax.rsqrt(squares * (k_scale * k_scale) + epsilon)
        key_unit = (raw * factor).astype(jnp.bfloat16)
        pre = pre_ref[h] * factor[:, :1]
        gate = pre[:, :hid]
        lin = pre[:, hid:]
        sigmoid, swish = silu_parts(gate)
        hidden = (swish * lin).astype(jnp.bfloat16)
        hidden_grad = hg_ref[h]
        d_gate = hidden_grad * lin * sigmoid * (1.0 + gate * (1.0 - sigmoid))
        d_lin = hidden_grad * swish
        for j, d_part in enumerate((d_gate, d_lin)):
            grad_in = dot(key_unit, d_part.astype(jnp.bfloat16), ((0,), (0,)))
            for half in range(2):
                grad[h, pl.ds((2 * j + half) * 128, 128)] = grad_in[
                    :, half * 128 : half * 128 + 128
                ].astype(jnp.bfloat16)
        grad[h, pl.ds(512, 256)] = dot(hidden, push_ref[h], ((0,), (0,))).astype(jnp.bfloat16)
        rc_copy(h).start()
        return carry

    lax.fori_loop(0, local_heads, grads, 0)

    scaling = math.log2(math.e) / math.sqrt(dim)

    def queries(h, carry):
        raw = q_ref[h].astype(jnp.float32) * q_scale * qg_ref[pl.ds(h, 1)]
        qt[h] = jnp.transpose(raw * scaling).astype(jnp.bfloat16)
        qu[h] = unit(raw.astype(jnp.bfloat16))
        return carry

    lax.fori_loop(0, local_heads, queries, 0)

    positions = t * rows + lax.broadcasted_iota(jnp.int32, (1, rows), 1)
    clip_first = jnp.zeros((1, rows), jnp.int32)
    clip_last = jnp.full((1, rows), total_tokens - 1, jnp.int32)
    for b in range(bd_ref.shape[0]):
        edge = bd_ref[b]
        clip_first = jnp.where(positions >= edge, jnp.maximum(clip_first, edge), clip_first)
        clip_last = jnp.where(positions < edge, jnp.minimum(clip_last, edge - 1), clip_last)

    def absorb(keys, values, off, first=False):
        scale = k_scale if first else scale_of(tot_all[off + 4][0:1])
        places = (t + off) * rows + lax.broadcasted_iota(jnp.int32, (rows, rows), 0)

        def one(h, carry):
            window = hw_ref[h]
            low = jnp.maximum(positions - window, clip_first)
            high = jnp.minimum(positions + window, clip_last)
            block = normed(keys[h], scale, kg_ref[pl.ds(h, 1)])
            scores = dot(block, qt[h])
            scores = jnp.where((places >= low) & (places <= high), scores, NEG)
            best = jnp.max(scores, axis=0, keepdims=True)
            if not first:
                best_old = m_ref[pl.ds(h, 1)]
                best = jnp.maximum(best, best_old)
            weights = jnp.exp2(scores - best)
            denom = jnp.sum(weights, axis=0, keepdims=True)
            product = dot(values[h], weights.astype(jnp.bfloat16), ((0,), (0,)))
            if not first:
                shrink = jnp.exp2(best_old - best)
                denom = denom + l_ref[pl.ds(h, 1)] * shrink
                product = product + acc[h] * shrink
            m_ref[pl.ds(h, 1)] = best
            l_ref[pl.ds(h, 1)] = denom
            acc[h] = product
            return carry

        lax.fori_loop(0, local_heads, one, 0)

    def absorb_slot(slot):
        absorb(kh.at[slot], vh.at[slot], slot_off[slot])

    def arrived(slot):
        k_copy[slot].wait_recv()
        v_copy[slot].wait_recv()

    def rows_of(ref, h, start, size):
        return ref[h, pl.ds(pl.multiple_of(start, size), size)].astype(jnp.float32)

    def ry_copy(h):
        return remote(s1.at[h], ry.at[h], ry_send.at[h], ry_recv.at[h], at_tok(y_peer))

    def rp_copy(h):
        return remote(s2.at[h], rp.at[h], rp_send.at[h], rp_recv.at[h], at_tok(pair))

    def core_stage(h, carry):
        rc_copy(h).wait_recv()
        away = (1 - yl) * 192
        s1[h] = (rows_of(grad, h, core * 384 + away, 192) + rows_of(rc, h, away, 192)).astype(
            jnp.bfloat16
        )
        ry_copy(h).start()
        return carry

    def so_far(h, which):
        return (
            rows_of(grad, h, core * 384 + yl * 192 + which * 96, 96)
            + rows_of(rc, h, yl * 192 + which * 96, 96)
            + rows_of(ry, h, which * 96, 96)
        )

    def y_stage(h, carry):
        ry_copy(h).wait_recv()
        s2[h] = so_far(h, 1 - zp).astype(jnp.bfloat16)
        rp_copy(h).start()
        return carry

    def pair_stage(h, carry):
        rp_copy(h).wait_recv()
        qb[pl.ds(pl.multiple_of(h * 96, 96), 96)] = (
            so_far(h, zp) + rp[h].astype(jnp.float32)
        ).astype(jnp.bfloat16)
        return carry

    def part_at(which):
        return pl.ds(pl.multiple_of(which * part, part), part)

    def rz_copy(i):
        other = (zo + i) % owners
        return remote(
            qb.at[part_at(other)],
            rz.at[zo],
            rz_send.at[other],
            rz_recv.at[zo],
            at_tok(z_peer(i)),
        )

    def rz_arrival(i):
        other = (zo + i) % owners
        return remote(
            qb.at[part_at(other)],
            rz.at[other],
            rz_send.at[other],
            rz_recv.at[other],
            at_tok(z_peer(i)),
        )

    pad_at = local_heads * 96
    qb[pl.ds(pad_at, EIGHTH - pad_at)] = jnp.zeros((EIGHTH - pad_at, dim), jnp.bfloat16)
    order = far_first(owners)

    here = core * 4 + yl * 2

    def shared(lane, which, send, recv, index, dev):
        piece = wsum.at[lane, part_at(which)]
        return remote(piece, piece, send.at[index], recv.at[index], at_tok(dev))

    def az_copy(i):
        piece = wsum.at[here + zp, part_at(zo)]
        return remote(
            piece, piece, az_send.at[(zo + i) % owners], az_recv.at[zo], at_tok(z_peer(i))
        )

    def az_arrival(i):
        other = (zo + i) % owners
        return shared(here + zp, other, az_send, az_recv, other, z_peer(i))

    def ap_copy(lane_pair, which):
        return shared(here + lane_pair, which, ap_send, ap_recv, which, pair)

    def ay_copy(lane_y, lane_pair, which):
        lane = core * 4 + lane_y * 2 + lane_pair
        return shared(lane, which, ay_send, ay_recv, lane_pair * owners + which, y_peer)

    def ac_copy(lane_core, lane_y, lane_pair, which):
        lane = lane_core * 4 + lane_y * 2 + lane_pair
        index = (lane_y * 2 + lane_pair) * owners + which
        return shared(lane, which, ac_send, ac_recv, index, partner)

    def ring(i):
        return (zo + i) % owners

    def arrived(slot):
        k_copy[slot].wait_recv()
        v_copy[slot].wait_recv()

    lax.fori_loop(0, local_heads, core_stage, 0)
    absorb(k_ref, v_ref, 0, first=True)
    lax.fori_loop(0, local_heads, y_stage, 0)
    for off in offsets:
        tot_copy(off).wait_recv()
    lax.fori_loop(0, local_heads, pair_stage, 0)
    for i in order:
        rz_copy(i).start()

    for slot in (1, 2):
        k_copy[slot].wait_recv()
    for slot in (0, 3, 4, 6):
        k_copy[slot].start()
    arrived(5)
    absorb_slot(5)
    for slot in (1, 2):
        v_copy[slot].wait_recv()
    for slot in (4, 6):
        v_copy[slot].start()
    absorb_slot(1)

    summed = qb[part_at(zo)].astype(jnp.float32)
    for i in order:
        rz_arrival(i).wait_recv()
        summed = summed + rz[ring(i)].astype(jnp.float32)
    wsum[here + zp, part_at(zo)] = summed.astype(jnp.bfloat16)
    for i in order:
        az_copy(i).start()
    ap_copy(zp, zo).start()
    ay_copy(yl, zp, zo).start()
    ac_copy(core, yl, zp, zo).start()
    for slot in (0, 3):
        v_copy[slot].start()

    absorb_slot(2)
    arrived(4)
    absorb_slot(4)

    for i in order:
        az_arrival(i).wait_recv()
        ap_copy(zp, ring(i)).start()
        ay_copy(yl, zp, ring(i)).start()
        ac_copy(core, yl, zp, ring(i)).start()
    for i in [0] + order:
        ap_copy(1 - zp, ring(i)).wait_recv()
        ay_copy(yl, 1 - zp, ring(i)).start()
        ac_copy(core, yl, 1 - zp, ring(i)).start()
    for lane_pair in (zp, 1 - zp):
        for i in [0] + order:
            ay_copy(1 - yl, lane_pair, ring(i)).wait_recv()
            ac_copy(core, 1 - yl, lane_pair, ring(i)).start()

    for slot in (0, 3):
        k_copy[slot].wait_recv()
    k_copy[7].start()
    arrived(6)
    absorb_slot(6)

    for lane_y in range(2):
        for lane_pair in range(2):
            for which in range(owners):
                ac_copy(1 - core, lane_y, lane_pair, which).wait_recv()

    def sums(h, first, size):
        pieces = []
        for piece in range(first // 32, (first + size) // 32):
            start = pl.multiple_of(h * 96 + (piece % 3) * 32, 32)
            pieces.append(wsum[piece // 3, pl.ds(start, 32)].astype(jnp.float32))
        return jnp.concatenate(pieces, axis=0)

    def renewed(h, base, first, size):
        base = base.astype(jnp.float32)
        updated = base - sums(h, first, size)
        norm = jnp.sqrt(jnp.sum(base * base, axis=0, keepdims=True))
        squares = jnp.sum(updated * updated, axis=0, keepdims=True)
        return (updated * (norm / jnp.sqrt(squares + epsilon))).astype(jnp.bfloat16)

    def apply_fast(h, carry):
        query_unit = qu[h]
        query_hidden = []
        for half in range(2):
            at = half * 128
            gate = dot(query_unit, renewed(h, fi_ref[h, :, at : at + 128], at, 128))
            lin = dot(
                query_unit,
                renewed(h, fi_ref[h, :, hid + at : hid + at + 128], 256 + at, 128),
            )
            query_hidden.append((silu_parts(gate)[1] * lin).astype(jnp.bfloat16))
        new_out = renewed(h, fo_ref[h], 512, hid)
        fast[h] = dot(jnp.concatenate(query_hidden, axis=1), new_out)
        return carry

    lax.fori_loop(0, local_heads, apply_fast, 0)

    for slot in (0, 3):
        v_copy[slot].wait_recv()
    v_copy[7].start()
    absorb_slot(0)
    absorb_slot(3)
    arrived(7)
    absorb_slot(7)

    def finish(h, carry):
        attended = jnp.transpose(acc[h] / l_ref[pl.ds(h, 1)])
        out_ref[h] = (attended + fast[h]).astype(jnp.bfloat16)
        return carry

    lax.fori_loop(0, local_heads, finish, 0)

    for i in range(1, n_head):
        ss_copy(i).wait_send()
    for off in offsets:
        tot_copy(off).wait_send()
    for slot in range(8):
        k_copy[slot].wait_send()
        v_copy[slot].wait_send()

    def sent(h, carry):
        rc_copy(h).wait_send()
        ry_copy(h).wait_send()
        rp_copy(h).wait_send()
        return carry

    lax.fori_loop(0, local_heads, sent, 0)
    for i in order:
        rz_copy(i).wait_send()
        az_copy(i).wait_send()
    for which in range(owners):
        ap_copy(zp, which).wait_send()
        for lane_pair in range(2):
            ay_copy(yl, lane_pair, which).wait_send()
            for lane_y in range(2):
                ac_copy(core, lane_y, lane_pair, which).wait_send()


def body(q, k, v, q_gain, k_gain, rate_in, rate_out, fast_in, fast_out, half_window, boundaries):
    rows, heads, dim = q.shape
    n_tok = lax.axis_size("tok")
    n_head = lax.axis_size("head")
    owners = n_tok // 8
    part = EIGHTH // owners
    bf16 = jnp.bfloat16
    f32 = jnp.float32
    vmem = pl.BlockSpec(memory_space=pltpu.VMEM)
    smem = pl.BlockSpec(memory_space=pltpu.SMEM)
    dma = pltpu.SemaphoreType.DMA

    def call(*refs):
        kernel(heads * n_head, n_tok, n_head, *refs)

    result = pl.pallas_call(
        call,
        out_shape=jax.ShapeDtypeStruct((heads, rows, dim), bf16),
        in_specs=[vmem] * 9 + [smem] * 2,
        out_specs=vmem,
        scratch_shapes=[
            pltpu.VMEM((8, heads, rows, dim), bf16),
            pltpu.VMEM((8, heads, rows, dim), bf16),
            pltpu.VMEM((8, rows), f32),
            pltpu.VMEM((n_head, 8, rows), f32),
            pltpu.VMEM((9, 8, rows), f32),
            pltpu.VMEM((heads, dim, rows), bf16),
            pltpu.VMEM((heads, rows, dim), bf16),
            pltpu.VMEM((8, rows), f32),
            pltpu.VMEM((8, rows), f32),
            pltpu.VMEM((heads, dim, rows), f32),
            pltpu.VMEM((heads, rows, 512), f32),
            pltpu.VMEM((heads, rows, dim), bf16),
            pltpu.VMEM((heads, rows, 256), f32),
            pltpu.VMEM((heads, HEAD_ROWS, dim), bf16),
            pltpu.VMEM((heads, HEAD_ROWS // 2, dim), bf16),
            pltpu.VMEM((heads, HEAD_ROWS // 4, dim), bf16),
            pltpu.VMEM((heads, HEAD_ROWS // 4, dim), bf16),
            pltpu.VMEM((heads, HEAD_ROWS // 8, dim), bf16),
            pltpu.VMEM((heads, HEAD_ROWS // 8, dim), bf16),
            pltpu.VMEM((EIGHTH, dim), bf16),
            pltpu.VMEM((owners, part, dim), bf16),
            pltpu.VMEM((8, EIGHTH, dim), bf16),
            pltpu.VMEM((heads, rows, dim), f32),
            dma((n_head,)),
            dma((n_head,)),
            dma((9,)),
            dma((9,)),
            dma((8,)),
            dma((8,)),
            dma((8,)),
            dma((8,)),
            dma((heads,)),
            dma((heads,)),
            dma((heads,)),
            dma((heads,)),
            dma((heads,)),
            dma((heads,)),
            dma((owners,)),
            dma((owners,)),
            dma((owners,)),
            dma((owners,)),
            dma((owners,)),
            dma((owners,)),
            dma((2 * owners,)),
            dma((2 * owners,)),
            dma((4 * owners,)),
            dma((4 * owners,)),
        ],
        compiler_params=pltpu.CompilerParams(
            collective_id=0, has_side_effects=True, vmem_limit_bytes=60 * 1024 * 1024
        ),
    )(
        jnp.transpose(q, (1, 0, 2)),
        jnp.transpose(k, (1, 0, 2)),
        jnp.transpose(v, (1, 0, 2)),
        q_gain,
        k_gain,
        rate_in,
        rate_out,
        fast_in,
        fast_out,
        half_window,
        boundaries,
    )
    return jnp.transpose(result, (1, 0, 2))


def solution(mesh):
    in_specs = (
        P("tok", "head", None),
        P("tok", "head", None),
        P("tok", "head", None),
        P("head", None),
        P("head", None),
        P("head", "tok"),
        P("head", "tok"),
        P("head", None, None),
        P("head", None, None),
        P("head"),
        P(),
    )
    out_specs = P("tok", "head", None)
    return jax.shard_map(body, mesh=mesh, in_specs=in_specs, out_specs=out_specs, check_vma=False)
```

```python
import math

import jax
import jax.numpy as jnp
from jax import lax
from jax.experimental import pallas as pl
from jax.experimental.pallas import tpu as pltpu
from jax.sharding import PartitionSpec as P

epsilon = 1e-06
MESH = pl.DeviceIdType.MESH
NEG = -1e30
HEAD_ROWS = 768
EIGHTH = 512


def far_first(n):
    return sorted(range(1, n), key=lambda i: (-min(i, n - i), i))


def rows_to_columns(row, lanes):
    return jnp.transpose(jnp.broadcast_to(row, (lanes, row.shape[1])))


def silu_parts(gate):
    sigmoid = 1.0 / (1.0 + jnp.exp(-gate))
    return sigmoid, gate * sigmoid


def dot(a, b, dims=((1,), (0,))):
    return lax.dot_general(a, b, (dims, ((), ())), preferred_element_type=jnp.float32)


def kernel(
    heads_all,
    n_tok,
    n_head,
    q_hbm,
    k_hbm,
    v_hbm,
    qg_hbm,
    kg_hbm,
    ri_hbm,
    ro_hbm,
    fi_hbm,
    fo_hbm,
    hw_ref,
    bd_ref,
    out_hbm,
    q_ref,
    k_ref,
    v_ref,
    qg_ref,
    kg_ref,
    ri_ref,
    ro_ref,
    fi_ref,
    fo_ref,
    out_ref,
    in_sem,
    out_sem,
    kh,
    vh,
    ss_loc,
    ss_all,
    tot_all,
    qt,
    qu,
    m_ref,
    l_ref,
    acc,
    pre_ref,
    push_ref,
    hg_ref,
    grad,
    rc,
    s1,
    ry,
    s2,
    rp,
    qb,
    rz,
    wsum,
    fast,
    ss_send,
    ss_recv,
    tot_send,
    tot_recv,
    hk_send,
    hk_recv,
    hv_send,
    hv_recv,
    rc_send,
    rc_recv,
    ry_send,
    ry_recv,
    rp_send,
    rp_recv,
    rz_send,
    rz_recv,
    az_send,
    az_recv,
    ap_send,
    ap_recv,
    ay_send,
    ay_recv,
    ac_send,
    ac_recv,
    token,
):
    local_heads, rows, dim = k_ref.shape
    hid = fo_ref.shape[1]
    total_tokens = rows * n_tok
    chips = n_tok // 2
    nz = chips // 2
    owners = nz // 2
    part = EIGHTH // owners
    t = lax.axis_index("tok")
    me_head = lax.axis_index("head")
    core = t % 2
    chip = t // 2
    z = chip % nz
    yl = chip // nz
    shifted = (z + core) % nz
    zp = shifted % 2
    zo = shifted // 2
    partner = t + 1 - 2 * core
    y_peer = (1 - yl) * (2 * nz) + z * 2 + core
    pair = yl * (2 * nz) + ((z + 1 - 2 * zp + nz) % nz) * 2 + core

    def z_peer(i):
        there = ((zo + i) % owners) * 2 + zp - core + nz
        return yl * (2 * nz) + (there % nz) * 2 + core

    def tok_ring(off):
        return (t + off + n_tok) % n_tok

    def at_tok(dev):
        return (dev, me_head)

    barrier = pltpu.get_barrier_semaphore()

    def greet(dev):
        pl.semaphore_signal(barrier, inc=1, device_id=dev, device_id_type=MESH)

    z_sides = sorted({1, owners - 1} - {0})
    for i in range(1, n_head):
        greet((t, (me_head + i) % n_head))
    for i in z_sides:
        greet(at_tok(z_peer(i)))
    for off in (1, 2, 3, 4):
        greet(at_tok(tok_ring(off)))
        greet(at_tok(tok_ring(-off)))
    greet(at_tok(y_peer))
    greet(at_tok(pair))

    loads = []
    for src, dst in (
        (k_hbm, k_ref),
        (q_hbm, q_ref),
        (kg_hbm, kg_ref),
        (fi_hbm, fi_ref),
        (v_hbm, v_ref),
        (ro_hbm, ro_ref),
        (ri_hbm, ri_ref),
        (fo_hbm, fo_ref),
        (qg_hbm, qg_ref),
    ):
        loads.append(pltpu.make_async_copy(src, dst, in_sem.at[len(loads)]))
        loads[-1].start()

    def remote(src, dst, send, recv, dev):
        return pltpu.make_async_remote_copy(
            src_ref=src,
            dst_ref=dst,
            send_sem=send,
            recv_sem=recv,
            device_id=dev,
            device_id_type=MESH,
        )

    pieces = ((0, 3), (3, local_heads - 3))

    def halo(ref, buf, send, recv, slot, dev):
        return [
            remote(
                ref.at[pl.ds(first, count)],
                buf.at[slot, pl.ds(first, count)],
                send.at[2 * slot + index],
                recv.at[2 * slot + index],
                at_tok(dev),
            )
            for index, (first, count) in enumerate(pieces)
        ]

    def start(copies, *which):
        for index in which or (0, 1):
            copies[index].start()

    def wait_recv(copies):
        for copy in copies:
            copy.wait_recv()

    k_copy = {}
    v_copy = {}
    far_src = 3 * (1 - core)
    routes = (
        (1, None, tok_ring(2)),
        (2, None, tok_ring(-2)),
        (0, 1, tok_ring(2)),
        (3, 2, tok_ring(-2)),
        (4, 1, partner),
        (5, None, partner),
        (6, 2, partner),
        (7, far_src, partner),
    )
    for slot, src, dev in routes:
        k_src = k_ref if src is None else kh.at[src]
        v_src = v_ref if src is None else vh.at[src]
        k_copy[slot] = halo(k_src, kh, hk_send, hk_recv, slot, dev)
        v_copy[slot] = halo(v_src, vh, hv_send, hv_recv, slot, dev)
    side = 1 - 2 * core
    slot_off = {0: -4, 1: -2, 2: 2, 3: 4, 4: side - 2, 5: side, 6: side + 2, 7: -3 * side}

    k_sq = jnp.zeros((rows, dim), jnp.float32)
    q_sq = jnp.zeros((rows, dim), jnp.float32)
    loads[0].wait()
    loads[1].wait()
    for h in range(local_heads):
        kf = k_ref[h].astype(jnp.float32)
        qf = q_ref[h].astype(jnp.float32)
        k_sq = k_sq + kf * kf
        q_sq = q_sq + qf * qf
    k_row = jnp.sum(jnp.transpose(k_sq), axis=0, keepdims=True)
    q_row = jnp.sum(jnp.transpose(q_sq), axis=0, keepdims=True)
    sub = lax.broadcasted_iota(jnp.int32, (8, rows), 0)
    ss_loc[...] = jnp.where(
        sub == 0, jnp.broadcast_to(k_row, (8, rows)), jnp.broadcast_to(q_row, (8, rows))
    )

    pl.semaphore_wait(barrier, len(z_sides) + (n_head - 1) + 8 + 2)
    rounds = max(owners // 2 - 1, 0)

    def tokens_out(step):
        if step < rounds:
            for side, i in enumerate(z_sides):
                pl.semaphore_signal(
                    token.at[2 * step + side],
                    inc=1,
                    device_id=at_tok(z_peer(i)),
                    device_id_type=MESH,
                )

    def tokens_in(step):
        if step < rounds:
            for side in range(len(z_sides)):
                pl.semaphore_wait(token.at[2 * step + side], 1)

    assert rounds <= 3

    def ss_copy(i):
        other = (me_head + i) % n_head
        return remote(
            ss_loc, ss_all.at[me_head], ss_send.at[other], ss_recv.at[me_head], (t, other)
        )

    def ss_arrival(i):
        other = (me_head + i) % n_head
        return remote(
            ss_loc, ss_all.at[other], ss_send.at[other], ss_recv.at[other], (t, other)
        )

    for i in range(1, n_head):
        ss_copy(i).start()
    for slot in (1, 2, 5):
        start(k_copy[slot])
    tokens_out(0)

    for load in loads[2:]:
        load.wait()

    def early(h, carry):
        key_gained = k_ref[h].astype(jnp.float32) * kg_ref[pl.ds(h, 1)]
        pre_ref[h] = dot(key_gained.astype(jnp.bfloat16), fi_ref[h])
        value = v_ref[h].astype(jnp.float32)
        push_ref[h] = (-rows_to_columns(ro_ref[pl.ds(h, 1)], dim) * value).astype(jnp.bfloat16)
        push_in = (-rows_to_columns(ri_ref[pl.ds(h, 1)], dim) * value).astype(jnp.bfloat16)
        hg_ref[h] = dot(push_in, fo_ref[h], ((1,), (1,)))
        return carry

    lax.fori_loop(0, local_heads, early, 0)
    for i in range(1, n_head):
        ss_arrival(i).wait_recv()
    total = ss_loc[...]
    for i in range(1, n_head):
        total = total + ss_all[(me_head + i) % n_head]
    tot_all[4] = total

    def tot_copy(off):
        return remote(
            tot_all.at[4],
            tot_all.at[4 - off],
            tot_send.at[4 - off],
            tot_recv.at[4 - off],
            at_tok(tok_ring(off)),
        )

    offsets = (1, -1, 2, -2, 3, -3, 4, -4)
    for off in offsets:
        tot_copy(off).start()
    for slot in (1, 2):
        start(v_copy[slot], 0)
    start(v_copy[5])

    inv_width = 1.0 / (heads_all * dim)

    def scale_of(sums_row):
        return rows_to_columns(lax.rsqrt(sums_row * inv_width + epsilon), dim)

    def normed(block, scale, gain):
        return (block.astype(jnp.float32) * scale * gain).astype(jnp.bfloat16)

    def unit(block):
        as_float = block.astype(jnp.float32)
        squares = jnp.sum(as_float * as_float, axis=1, keepdims=True)
        return (as_float * lax.rsqrt(squares + epsilon)).astype(jnp.bfloat16)

    k_scale = scale_of(total[0:1])
    q_scale = scale_of(total[1:2])

    def rc_copy(h):
        return remote(
            grad.at[h, pl.ds(pl.multiple_of((1 - core) * 384, 384), 384)],
            rc.at[h],
            rc_send.at[h],
            rc_recv.at[h],
            at_tok(partner),
        )

    def grads(h, carry):
        raw = k_ref[h].astype(jnp.float32) * kg_ref[pl.ds(h, 1)]
        squares = jnp.sum(raw * raw, axis=1, keepdims=True)
        factor = k_scale * lax.rsqrt(squares * (k_scale * k_scale) + epsilon)
        key_unit = (raw * factor).astype(jnp.bfloat16)
        pre = pre_ref[h] * factor[:, :1]
        gate = pre[:, :hid]
        lin = pre[:, hid:]
        sigmoid, swish = silu_parts(gate)
        hidden = (swish * lin).astype(jnp.bfloat16)
        hidden_grad = hg_ref[h]
        d_gate = hidden_grad * lin * sigmoid * (1.0 + gate * (1.0 - sigmoid))
        d_lin = hidden_grad * swish
        for j, d_part in enumerate((d_gate, d_lin)):
            grad_in = dot(key_unit, d_part.astype(jnp.bfloat16), ((0,), (0,)))
            for half in range(2):
                grad[h, pl.ds((2 * j + half) * 128, 128)] = grad_in[
                    :, half * 128 : half * 128 + 128
                ].astype(jnp.bfloat16)
        grad[h, pl.ds(512, 256)] = dot(hidden, push_ref[h], ((0,), (0,))).astype(jnp.bfloat16)
        rc_copy(h).start()
        return carry

    lax.fori_loop(0, local_heads, grads, 0)

    scaling = math.log2(math.e) / math.sqrt(dim)

    def queries(h, carry):
        raw = q_ref[h].astype(jnp.float32) * q_scale * qg_ref[pl.ds(h, 1)]
        qt[h] = jnp.transpose(raw * scaling).astype(jnp.bfloat16)
        qu[h] = unit(raw.astype(jnp.bfloat16))
        return carry

    positions = t * rows + lax.broadcasted_iota(jnp.int32, (1, rows), 1)
    clip_first = jnp.zeros((1, rows), jnp.int32)
    clip_last = jnp.full((1, rows), total_tokens - 1, jnp.int32)
    for b in range(bd_ref.shape[0]):
        edge = bd_ref[b]
        clip_first = jnp.where(positions >= edge, jnp.maximum(clip_first, edge), clip_first)
        clip_last = jnp.where(positions < edge, jnp.minimum(clip_last, edge - 1), clip_last)

    def absorb(keys, values, off, first=False):
        scale = k_scale if first else scale_of(tot_all[off + 4][0:1])
        places = (t + off) * rows + lax.broadcasted_iota(jnp.int32, (rows, rows), 0)

        def one(h, carry):
            window = hw_ref[h]
            low = jnp.maximum(positions - window, clip_first)
            high = jnp.minimum(positions + window, clip_last)
            block = normed(keys[h], scale, kg_ref[pl.ds(h, 1)])
            scores = dot(block, qt[h])
            scores = jnp.where((places >= low) & (places <= high), scores, NEG)
            best = jnp.max(scores, axis=0, keepdims=True)
            if not first:
                best_old = m_ref[pl.ds(h, 1)]
                best = jnp.maximum(best, best_old)
            weights = jnp.exp2(scores - best)
            denom = jnp.sum(weights, axis=0, keepdims=True)
            product = dot(values[h], weights.astype(jnp.bfloat16), ((0,), (0,)))
            if not first:
                shrink = jnp.exp2(best_old - best)
                denom = denom + l_ref[pl.ds(h, 1)] * shrink
                product = product + acc[h] * shrink
            m_ref[pl.ds(h, 1)] = best
            l_ref[pl.ds(h, 1)] = denom
            acc[h] = product
            return carry

        lax.fori_loop(0, local_heads, one, 0, unroll=True)

    def absorb_slot(slot):
        absorb(kh.at[slot], vh.at[slot], slot_off[slot])

    def arrived(slot):
        k_copy[slot].wait_recv()
        v_copy[slot].wait_recv()

    def rows_of(ref, h, start, size):
        return ref[h, pl.ds(pl.multiple_of(start, size), size)].astype(jnp.float32)

    def ry_copy(h):
        return remote(s1.at[h], ry.at[h], ry_send.at[h], ry_recv.at[h], at_tok(y_peer))

    def rp_copy(h):
        return remote(s2.at[h], rp.at[h], rp_send.at[h], rp_recv.at[h], at_tok(pair))

    def core_stage(h, carry):
        rc_copy(h).wait_recv()
        away = (1 - yl) * 192
        s1[h] = (rows_of(grad, h, core * 384 + away, 192) + rows_of(rc, h, away, 192)).astype(
            jnp.bfloat16
        )
        ry_copy(h).start()
        return carry

    def so_far(h, which):
        return (
            rows_of(grad, h, core * 384 + yl * 192 + which * 96, 96)
            + rows_of(rc, h, yl * 192 + which * 96, 96)
            + rows_of(ry, h, which * 96, 96)
        )

    def y_stage(h, carry):
        ry_copy(h).wait_recv()
        s2[h] = so_far(h, 1 - zp).astype(jnp.bfloat16)
        rp_copy(h).start()
        return carry

    def pair_stage(h, carry):
        rp_copy(h).wait_recv()
        qb[pl.ds(pl.multiple_of(h * 96, 96), 96)] = (
            so_far(h, zp) + rp[h].astype(jnp.float32)
        ).astype(jnp.bfloat16)
        return carry

    def part_at(which):
        return pl.ds(pl.multiple_of(which * part, part), part)

    def rz_copy(i):
        other = (zo + i) % owners
        return remote(
            qb.at[part_at(other)],
            rz.at[zo],
            rz_send.at[other],
            rz_recv.at[zo],
            at_tok(z_peer(i)),
        )

    def rz_arrival(i):
        other = (zo + i) % owners
        return remote(
            qb.at[part_at(other)],
            rz.at[other],
            rz_send.at[other],
            rz_recv.at[other],
            at_tok(z_peer(i)),
        )

    pad_at = local_heads * 96
    qb[pl.ds(pad_at, EIGHTH - pad_at)] = jnp.zeros((EIGHTH - pad_at, dim), jnp.bfloat16)
    order = far_first(owners)

    here = core * 4 + yl * 2

    def shared(lane, which, send, recv, index, dev):
        piece = wsum.at[lane, part_at(which)]
        return remote(piece, piece, send.at[index], recv.at[index], at_tok(dev))

    def az_copy(i):
        piece = wsum.at[here + zp, part_at(zo)]
        return remote(
            piece, piece, az_send.at[(zo + i) % owners], az_recv.at[zo], at_tok(z_peer(i))
        )

    def az_arrival(i):
        other = (zo + i) % owners
        return shared(here + zp, other, az_send, az_recv, other, z_peer(i))

    def ap_copy(lane_pair, which):
        return shared(here + lane_pair, which, ap_send, ap_recv, which, pair)

    def ay_copy(lane_y, lane_pair, which):
        lane = core * 4 + lane_y * 2 + lane_pair
        return shared(lane, which, ay_send, ay_recv, lane_pair * owners + which, y_peer)

    def ac_copy(lane_core, lane_y, lane_pair, which):
        lane = lane_core * 4 + lane_y * 2 + lane_pair
        index = (lane_y * 2 + lane_pair) * owners + which
        return shared(lane, which, ac_send, ac_recv, index, partner)

    def ring(i):
        return (zo + i) % owners

    def arrived(slot):
        wait_recv(k_copy[slot])
        wait_recv(v_copy[slot])

    lax.fori_loop(0, local_heads, core_stage, 0)
    tokens_in(0)
    tokens_out(1)
    lax.fori_loop(0, local_heads, queries, 0)
    absorb(k_ref, v_ref, 0, first=True)
    tokens_in(1)
    tokens_out(2)
    lax.fori_loop(0, local_heads, y_stage, 0)
    for slot in (1, 2):
        start(v_copy[slot], 1)
    for off in offsets:
        tot_copy(off).wait_recv()
    arrived(5)
    absorb_slot(5)
    lax.fori_loop(0, local_heads, pair_stage, 0)
    tokens_in(2)
    for i in order:
        rz_copy(i).start()

    for slot in (1, 2):
        wait_recv(k_copy[slot])
    for slot in (0, 3):
        start(k_copy[slot])
    for slot in (4, 6):
        start(k_copy[slot])
    for slot in (1, 2):
        wait_recv(v_copy[slot])
    for slot in (4, 6):
        start(v_copy[slot])
    absorb_slot(1)
    absorb_slot(2)
    arrived(4)
    absorb_slot(4)

    summed = qb[part_at(zo)].astype(jnp.float32)
    for i in order:
        rz_arrival(i).wait_recv()
        summed = summed + rz[ring(i)].astype(jnp.float32)
    wsum[here + zp, part_at(zo)] = summed.astype(jnp.bfloat16)
    for i in order:
        az_copy(i).start()
    ap_copy(zp, zo).start()
    ay_copy(yl, zp, zo).start()
    ac_copy(core, yl, zp, zo).start()
    for slot in (0, 3):
        start(v_copy[slot], 0)

    arrived(6)
    absorb_slot(6)

    for i in order:
        az_arrival(i).wait_recv()
        ap_copy(zp, ring(i)).start()
        ay_copy(yl, zp, ring(i)).start()
        ac_copy(core, yl, zp, ring(i)).start()
    for slot in (0, 3):
        start(v_copy[slot], 1)
    for i in [0] + order:
        ap_copy(1 - zp, ring(i)).wait_recv()
        ay_copy(yl, 1 - zp, ring(i)).start()
        ac_copy(core, yl, 1 - zp, ring(i)).start()
    for slot in (0, 3):
        wait_recv(k_copy[slot])
    start(k_copy[7])
    for lane_pair in (zp, 1 - zp):
        for i in [0] + order:
            ay_copy(1 - yl, lane_pair, ring(i)).wait_recv()
            ac_copy(core, 1 - yl, lane_pair, ring(i)).start()

    for slot in (0, 3):
        wait_recv(v_copy[slot])
    start(v_copy[7])
    absorb_slot(0)
    absorb_slot(3)
    for lane_y in range(2):
        for lane_pair in range(2):
            for which in range(owners):
                ac_copy(1 - core, lane_y, lane_pair, which).wait_recv()

    def sums(h, first, size):
        pieces = []
        for piece in range(first // 32, (first + size) // 32):
            start = pl.multiple_of(h * 96 + (piece % 3) * 32, 32)
            pieces.append(wsum[piece // 3, pl.ds(start, 32)].astype(jnp.float32))
        return jnp.concatenate(pieces, axis=0)

    def renewed(h, base, first, size):
        base = base.astype(jnp.float32)
        updated = base - sums(h, first, size)
        norm = jnp.sqrt(jnp.sum(base * base, axis=0, keepdims=True))
        squares = jnp.sum(updated * updated, axis=0, keepdims=True)
        return (updated * (norm / jnp.sqrt(squares + epsilon))).astype(jnp.bfloat16)

    def apply_fast(h, carry):
        query_unit = qu[h]
        query_hidden = []
        for half in range(2):
            at = half * 128
            gate = dot(query_unit, renewed(h, fi_ref[h, :, at : at + 128], at, 128))
            lin = dot(
                query_unit,
                renewed(h, fi_ref[h, :, hid + at : hid + at + 128], 256 + at, 128),
            )
            query_hidden.append((silu_parts(gate)[1] * lin).astype(jnp.bfloat16))
        new_out = renewed(h, fo_ref[h], 512, hid)
        fast[h] = dot(jnp.concatenate(query_hidden, axis=1), new_out)
        return carry

    def finish(h, carry):
        attended = jnp.transpose(acc[h] / l_ref[pl.ds(h, 1)])
        out_ref[h] = (attended + fast[h]).astype(jnp.bfloat16)
        return carry

    def out_copy(h):
        return pltpu.make_async_copy(out_ref.at[h], out_hbm.at[h], out_sem.at[h])

    lax.fori_loop(0, local_heads, apply_fast, 0, unroll=True)
    arrived(7)
    absorb_slot(7)
    lax.fori_loop(0, local_heads, finish, 0, unroll=True)

    for i in range(1, n_head):
        ss_copy(i).wait_send()
    for off in offsets:
        tot_copy(off).wait_send()
    for slot in range(8):
        for copy in k_copy[slot] + v_copy[slot]:
            copy.wait_send()

    def sent(h, carry):
        rc_copy(h).wait_send()
        ry_copy(h).wait_send()
        rp_copy(h).wait_send()
        return carry

    lax.fori_loop(0, local_heads, sent, 0)
    for i in order:
        rz_copy(i).wait_send()
        az_copy(i).wait_send()
    for which in range(owners):
        ap_copy(zp, which).wait_send()
        for lane_pair in range(2):
            ay_copy(yl, lane_pair, which).wait_send()
            for lane_y in range(2):
                ac_copy(core, lane_y, lane_pair, which).wait_send()
    for h in range(local_heads):
        out_copy(h).start()
    for h in range(local_heads):
        out_copy(h).wait()


def body(q, k, v, q_gain, k_gain, rate_in, rate_out, fast_in, fast_out, half_window, boundaries):
    rows, heads, dim = q.shape
    n_tok = lax.axis_size("tok")
    n_head = lax.axis_size("head")
    owners = n_tok // 8
    part = EIGHTH // owners
    bf16 = jnp.bfloat16
    f32 = jnp.float32
    hbm = pl.BlockSpec(memory_space=pl.ANY)
    smem = pl.BlockSpec(memory_space=pltpu.SMEM)
    dma = pltpu.SemaphoreType.DMA

    def call(*refs):
        kernel(heads * n_head, n_tok, n_head, *refs)

    result = pl.pallas_call(
        call,
        out_shape=jax.ShapeDtypeStruct((heads, rows, dim), bf16),
        in_specs=[hbm] * 9 + [smem] * 2,
        out_specs=hbm,
        scratch_shapes=[
            pltpu.VMEM((heads, rows, dim), bf16),
            pltpu.VMEM((heads, rows, dim), bf16),
            pltpu.VMEM((heads, rows, dim), bf16),
            pltpu.VMEM((heads, dim), f32),
            pltpu.VMEM((heads, dim), f32),
            pltpu.VMEM((heads, rows), f32),
            pltpu.VMEM((heads, rows), f32),
            pltpu.VMEM((heads, dim, 512), bf16),
            pltpu.VMEM((heads, 256, dim), bf16),
            pltpu.VMEM((heads, rows, dim), bf16),
            dma((9,)),
            dma((heads,)),
            pltpu.VMEM((8, heads, rows, dim), bf16),
            pltpu.VMEM((8, heads, rows, dim), bf16),
            pltpu.VMEM((8, rows), f32),
            pltpu.VMEM((n_head, 8, rows), f32),
            pltpu.VMEM((9, 8, rows), f32),
            pltpu.VMEM((heads, dim, rows), bf16),
            pltpu.VMEM((heads, rows, dim), bf16),
            pltpu.VMEM((8, rows), f32),
            pltpu.VMEM((8, rows), f32),
            pltpu.VMEM((heads, dim, rows), f32),
            pltpu.VMEM((heads, rows, 512), f32),
            pltpu.VMEM((heads, rows, dim), bf16),
            pltpu.VMEM((heads, rows, 256), f32),
            pltpu.VMEM((heads, HEAD_ROWS, dim), bf16),
            pltpu.VMEM((heads, HEAD_ROWS // 2, dim), bf16),
            pltpu.VMEM((heads, HEAD_ROWS // 4, dim), bf16),
            pltpu.VMEM((heads, HEAD_ROWS // 4, dim), bf16),
            pltpu.VMEM((heads, HEAD_ROWS // 8, dim), bf16),
            pltpu.VMEM((heads, HEAD_ROWS // 8, dim), bf16),
            pltpu.VMEM((EIGHTH, dim), bf16),
            pltpu.VMEM((owners, part, dim), bf16),
            pltpu.VMEM((8, EIGHTH, dim), bf16),
            pltpu.VMEM((heads, rows, dim), f32),
            dma((n_head,)),
            dma((n_head,)),
            dma((9,)),
            dma((9,)),
            dma((16,)),
            dma((16,)),
            dma((16,)),
            dma((16,)),
            dma((heads,)),
            dma((heads,)),
            dma((heads,)),
            dma((heads,)),
            dma((heads,)),
            dma((heads,)),
            dma((owners,)),
            dma((owners,)),
            dma((owners,)),
            dma((owners,)),
            dma((owners,)),
            dma((owners,)),
            dma((2 * owners,)),
            dma((2 * owners,)),
            dma((4 * owners,)),
            dma((4 * owners,)),
            pltpu.SemaphoreType.REGULAR((6,)),
        ],
        compiler_params=pltpu.CompilerParams(
            collective_id=0, has_side_effects=True, vmem_limit_bytes=60 * 1024 * 1024
        ),
    )(
        jnp.transpose(q, (1, 0, 2)),
        jnp.transpose(k, (1, 0, 2)),
        jnp.transpose(v, (1, 0, 2)),
        q_gain,
        k_gain,
        rate_in,
        rate_out,
        fast_in,
        fast_out,
        half_window,
        boundaries,
    )
    return jnp.transpose(result, (1, 0, 2))


def solution(mesh):
    in_specs = (
        P("tok", "head", None),
        P("tok", "head", None),
        P("tok", "head", None),
        P("head", None),
        P("head", None),
        P("head", "tok"),
        P("head", "tok"),
        P("head", None, None),
        P("head", None, None),
        P("head"),
        P(),
    )
    out_specs = P("tok", "head", None)
    return jax.shard_map(body, mesh=mesh, in_specs=in_specs, out_specs=out_specs, check_vma=False)
```

```python
import math

import jax
import jax.numpy as jnp
from jax import lax
from jax.experimental import pallas as pl
from jax.experimental.pallas import tpu as pltpu
from jax.sharding import PartitionSpec as P

epsilon = 1e-06
MESH = pl.DeviceIdType.MESH
NEG = -1e30
HEAD_ROWS = 768
EIGHTH = 512


def far_first(n):
    return sorted(range(1, n), key=lambda i: (-min(i, n - i), i))


def rows_to_columns(row, lanes):
    return jnp.transpose(jnp.broadcast_to(row, (lanes, row.shape[1])))


def silu_parts(gate):
    sigmoid = 1.0 / (1.0 + jnp.exp(-gate))
    return sigmoid, gate * sigmoid


def dot(a, b, dims=((1,), (0,))):
    return lax.dot_general(a, b, (dims, ((), ())), preferred_element_type=jnp.float32)


def kernel(
    heads_all,
    n_tok,
    n_head,
    q_hbm,
    k_hbm,
    v_hbm,
    qg_hbm,
    kg_hbm,
    ri_hbm,
    ro_hbm,
    fi_hbm,
    fo_hbm,
    hw_ref,
    bd_ref,
    out_hbm,
    q_ref,
    k_ref,
    v_ref,
    qg_ref,
    kg_ref,
    ri_ref,
    ro_ref,
    fi_ref,
    fo_ref,
    out_ref,
    in_sem,
    out_sem,
    kh,
    vh,
    ss_loc,
    ss_all,
    tot_all,
    qt,
    qu,
    m_ref,
    l_ref,
    acc,
    pre_ref,
    push_ref,
    hg_ref,
    grad,
    rc,
    s1,
    ry,
    s2,
    rp,
    qb,
    rz,
    wsum,
    fast,
    ss_send,
    ss_recv,
    tot_send,
    tot_recv,
    hk_send,
    hk_recv,
    hv_send,
    hv_recv,
    rc_send,
    rc_recv,
    ry_send,
    ry_recv,
    rp_send,
    rp_recv,
    rz_send,
    rz_recv,
    az_send,
    az_recv,
    ap_send,
    ap_recv,
    ay_send,
    ay_recv,
    ac_send,
    ac_recv,
    token,
):
    local_heads, rows, dim = k_ref.shape
    hid = fo_ref.shape[1]
    total_tokens = rows * n_tok
    chips = n_tok // 2
    nz = chips // 2
    owners = nz // 2
    part = EIGHTH // owners
    t = lax.axis_index("tok")
    me_head = lax.axis_index("head")
    core = t % 2
    chip = t // 2
    z = chip % nz
    yl = chip // nz
    shifted = (z + core) % nz
    zp = shifted % 2
    zo = shifted // 2
    partner = t + 1 - 2 * core
    y_peer = (1 - yl) * (2 * nz) + z * 2 + core
    pair = yl * (2 * nz) + ((z + 1 - 2 * zp + nz) % nz) * 2 + core

    def z_peer(i):
        there = ((zo + i) % owners) * 2 + zp - core + nz
        return yl * (2 * nz) + (there % nz) * 2 + core

    def tok_ring(off):
        return (t + off + n_tok) % n_tok

    def at_tok(dev):
        return (dev, me_head)

    barrier = pltpu.get_barrier_semaphore()

    def greet(dev):
        pl.semaphore_signal(barrier, inc=1, device_id=dev, device_id_type=MESH)

    z_sides = sorted({1, owners - 1} - {0})
    for i in range(1, n_head):
        greet((t, (me_head + i) % n_head))
    for i in z_sides:
        greet(at_tok(z_peer(i)))
    for off in (1, 2, 3, 4):
        greet(at_tok(tok_ring(off)))
        greet(at_tok(tok_ring(-off)))
    greet(at_tok(y_peer))
    greet(at_tok(pair))

    loads = []
    for src, dst in (
        (k_hbm, k_ref),
        (q_hbm, q_ref),
        (kg_hbm, kg_ref),
        (fi_hbm, fi_ref),
        (v_hbm, v_ref),
        (ro_hbm, ro_ref),
        (ri_hbm, ri_ref),
        (fo_hbm, fo_ref),
        (qg_hbm, qg_ref),
    ):
        loads.append(pltpu.make_async_copy(src, dst, in_sem.at[len(loads)]))
        loads[-1].start()

    def remote(src, dst, send, recv, dev):
        return pltpu.make_async_remote_copy(
            src_ref=src,
            dst_ref=dst,
            send_sem=send,
            recv_sem=recv,
            device_id=dev,
            device_id_type=MESH,
        )

    pieces = ((0, 3), (3, local_heads - 3))

    def halo(ref, buf, send, recv, slot, dev):
        return [
            remote(
                ref.at[pl.ds(first, count)],
                buf.at[slot, pl.ds(first, count)],
                send.at[2 * slot + index],
                recv.at[2 * slot + index],
                at_tok(dev),
            )
            for index, (first, count) in enumerate(pieces)
        ]

    def start(copies, *which):
        for index in which or (0, 1):
            copies[index].start()

    def wait_recv(copies):
        for copy in copies:
            copy.wait_recv()

    k_copy = {}
    v_copy = {}
    far_src = 3 * (1 - core)
    routes = (
        (1, None, tok_ring(2)),
        (2, None, tok_ring(-2)),
        (0, 1, tok_ring(2)),
        (3, 2, tok_ring(-2)),
        (4, 1, partner),
        (5, None, partner),
        (6, 2, partner),
        (7, far_src, partner),
    )
    for slot, src, dev in routes:
        k_src = k_ref if src is None else kh.at[src]
        v_src = v_ref if src is None else vh.at[src]
        k_copy[slot] = halo(k_src, kh, hk_send, hk_recv, slot, dev)
        v_copy[slot] = halo(v_src, vh, hv_send, hv_recv, slot, dev)
    side = 1 - 2 * core
    slot_off = {0: -4, 1: -2, 2: 2, 3: 4, 4: side - 2, 5: side, 6: side + 2, 7: -3 * side}

    k_sq = jnp.zeros((rows, dim), jnp.float32)
    q_sq = jnp.zeros((rows, dim), jnp.float32)
    loads[0].wait()
    loads[1].wait()
    for h in range(local_heads):
        kf = k_ref[h].astype(jnp.float32)
        qf = q_ref[h].astype(jnp.float32)
        k_sq = k_sq + kf * kf
        q_sq = q_sq + qf * qf
    k_row = jnp.sum(jnp.transpose(k_sq), axis=0, keepdims=True)
    q_row = jnp.sum(jnp.transpose(q_sq), axis=0, keepdims=True)
    sub = lax.broadcasted_iota(jnp.int32, (8, rows), 0)
    ss_loc[...] = jnp.where(
        sub == 0, jnp.broadcast_to(k_row, (8, rows)), jnp.broadcast_to(q_row, (8, rows))
    )

    pl.semaphore_wait(barrier, len(z_sides) + (n_head - 1) + 8 + 2)
    rounds = max(owners // 2 - 1, 0)

    def tokens_out(step):
        if step < rounds:
            for side, i in enumerate(z_sides):
                pl.semaphore_signal(
                    token.at[2 * step + side],
                    inc=1,
                    device_id=at_tok(z_peer(i)),
                    device_id_type=MESH,
                )

    def tokens_in(step):
        if step < rounds:
            for side in range(len(z_sides)):
                pl.semaphore_wait(token.at[2 * step + side], 1)

    assert rounds <= 3

    def ss_copy(i):
        other = (me_head + i) % n_head
        return remote(
            ss_loc, ss_all.at[me_head], ss_send.at[other], ss_recv.at[me_head], (t, other)
        )

    def ss_arrival(i):
        other = (me_head + i) % n_head
        return remote(
            ss_loc, ss_all.at[other], ss_send.at[other], ss_recv.at[other], (t, other)
        )

    for i in range(1, n_head):
        ss_copy(i).start()
    for slot in (1, 2, 5):
        start(k_copy[slot])
    tokens_out(0)

    for load in loads[2:]:
        load.wait()

    def early(h, carry):
        key_gained = k_ref[h].astype(jnp.float32) * kg_ref[pl.ds(h, 1)]
        pre_ref[h] = dot(key_gained.astype(jnp.bfloat16), fi_ref[h])
        value = v_ref[h].astype(jnp.float32)
        push_ref[h] = (-rows_to_columns(ro_ref[pl.ds(h, 1)], dim) * value).astype(jnp.bfloat16)
        push_in = (-rows_to_columns(ri_ref[pl.ds(h, 1)], dim) * value).astype(jnp.bfloat16)
        hg_ref[h] = dot(push_in, fo_ref[h], ((1,), (1,)))
        return carry

    lax.fori_loop(0, local_heads, early, 0)
    for i in range(1, n_head):
        ss_arrival(i).wait_recv()
    total = ss_loc[...]
    for i in range(1, n_head):
        total = total + ss_all[(me_head + i) % n_head]
    tot_all[4] = total

    def tot_copy(off):
        return remote(
            tot_all.at[4],
            tot_all.at[4 - off],
            tot_send.at[4 - off],
            tot_recv.at[4 - off],
            at_tok(tok_ring(off)),
        )

    offsets = (1, -1, 2, -2, 3, -3, 4, -4)
    for off in offsets:
        tot_copy(off).start()
    for slot in (1, 2):
        start(v_copy[slot], 0)
    start(v_copy[5])

    inv_width = 1.0 / (heads_all * dim)

    def scale_of(sums_row):
        return rows_to_columns(lax.rsqrt(sums_row * inv_width + epsilon), dim)

    def normed(block, scale, gain):
        return (block.astype(jnp.float32) * scale * gain).astype(jnp.bfloat16)

    def unit(block):
        as_float = block.astype(jnp.float32)
        squares = jnp.sum(as_float * as_float, axis=1, keepdims=True)
        return (as_float * lax.rsqrt(squares + epsilon)).astype(jnp.bfloat16)

    k_scale = scale_of(total[0:1])
    q_scale = scale_of(total[1:2])

    def rc_copy(h):
        return remote(
            grad.at[h, pl.ds(pl.multiple_of((1 - core) * 384, 384), 384)],
            rc.at[h],
            rc_send.at[h],
            rc_recv.at[h],
            at_tok(partner),
        )

    def grads(h, carry):
        raw = k_ref[h].astype(jnp.float32) * kg_ref[pl.ds(h, 1)]
        squares = jnp.sum(raw * raw, axis=1, keepdims=True)
        factor = k_scale * lax.rsqrt(squares * (k_scale * k_scale) + epsilon)
        key_unit = (raw * factor).astype(jnp.bfloat16)
        pre = pre_ref[h] * factor[:, :1]
        gate = pre[:, :hid]
        lin = pre[:, hid:]
        sigmoid, swish = silu_parts(gate)
        hidden = (swish * lin).astype(jnp.bfloat16)
        hidden_grad = hg_ref[h]
        d_gate = hidden_grad * lin * sigmoid * (1.0 + gate * (1.0 - sigmoid))
        d_lin = hidden_grad * swish
        for j, d_part in enumerate((d_gate, d_lin)):
            grad_in = dot(key_unit, d_part.astype(jnp.bfloat16), ((0,), (0,)))
            for half in range(2):
                grad[h, pl.ds((2 * j + half) * 128, 128)] = grad_in[
                    :, half * 128 : half * 128 + 128
                ].astype(jnp.bfloat16)
        grad[h, pl.ds(512, 256)] = dot(hidden, push_ref[h], ((0,), (0,))).astype(jnp.bfloat16)
        rc_copy(h).start()
        return carry

    lax.fori_loop(0, local_heads, grads, 0)

    scaling = math.log2(math.e) / math.sqrt(dim)

    def queries(h, carry):
        raw = q_ref[h].astype(jnp.float32) * q_scale * qg_ref[pl.ds(h, 1)]
        qt[h] = jnp.transpose(raw * scaling).astype(jnp.bfloat16)
        qu[h] = unit(raw.astype(jnp.bfloat16))
        return carry

    positions = t * rows + lax.broadcasted_iota(jnp.int32, (1, rows), 1)
    clip_first = jnp.zeros((1, rows), jnp.int32)
    clip_last = jnp.full((1, rows), total_tokens - 1, jnp.int32)
    for b in range(bd_ref.shape[0]):
        edge = bd_ref[b]
        clip_first = jnp.where(positions >= edge, jnp.maximum(clip_first, edge), clip_first)
        clip_last = jnp.where(positions < edge, jnp.minimum(clip_last, edge - 1), clip_last)

    def absorb(keys, values, off, first=False, which=None):
        scale = k_scale if first else scale_of(tot_all[off + 4][0:1])
        places = (t + off) * rows + lax.broadcasted_iota(jnp.int32, (rows, rows), 0)

        def one(h, carry):
            window = hw_ref[h]
            low = jnp.maximum(positions - window, clip_first)
            high = jnp.minimum(positions + window, clip_last)
            block = normed(keys[h], scale, kg_ref[pl.ds(h, 1)])
            scores = dot(block, qt[h])
            scores = jnp.where((places >= low) & (places <= high), scores, NEG)
            best = jnp.max(scores, axis=0, keepdims=True)
            if not first:
                best_old = m_ref[pl.ds(h, 1)]
                best = jnp.maximum(best, best_old)
            weights = jnp.exp2(scores - best)
            denom = jnp.sum(weights, axis=0, keepdims=True)
            product = dot(values[h], weights.astype(jnp.bfloat16), ((0,), (0,)))
            if not first:
                shrink = jnp.exp2(best_old - best)
                denom = denom + l_ref[pl.ds(h, 1)] * shrink
                product = product + acc[h] * shrink
            m_ref[pl.ds(h, 1)] = best
            l_ref[pl.ds(h, 1)] = denom
            acc[h] = product
            return carry

        low_head, count = (0, local_heads) if which is None else pieces[which]
        lax.fori_loop(low_head, low_head + count, one, 0, unroll=True)

    def absorb_slot(slot, which=None):
        absorb(kh.at[slot], vh.at[slot], slot_off[slot], which=which)

    def arrived(slot):
        k_copy[slot].wait_recv()
        v_copy[slot].wait_recv()

    def rows_of(ref, h, start, size):
        return ref[h, pl.ds(pl.multiple_of(start, size), size)].astype(jnp.float32)

    def ry_copy(h):
        return remote(s1.at[h], ry.at[h], ry_send.at[h], ry_recv.at[h], at_tok(y_peer))

    def rp_copy(h):
        return remote(s2.at[h], rp.at[h], rp_send.at[h], rp_recv.at[h], at_tok(pair))

    def core_stage(h, carry):
        rc_copy(h).wait_recv()
        away = (1 - yl) * 192
        s1[h] = (rows_of(grad, h, core * 384 + away, 192) + rows_of(rc, h, away, 192)).astype(
            jnp.bfloat16
        )
        ry_copy(h).start()
        return carry

    def so_far(h, which):
        return (
            rows_of(grad, h, core * 384 + yl * 192 + which * 96, 96)
            + rows_of(rc, h, yl * 192 + which * 96, 96)
            + rows_of(ry, h, which * 96, 96)
        )

    def y_stage(h, carry):
        ry_copy(h).wait_recv()
        s2[h] = so_far(h, 1 - zp).astype(jnp.bfloat16)
        rp_copy(h).start()
        return carry

    def pair_stage(h, carry):
        rp_copy(h).wait_recv()
        qb[pl.ds(pl.multiple_of(h * 96, 96), 96)] = (
            so_far(h, zp) + rp[h].astype(jnp.float32)
        ).astype(jnp.bfloat16)
        return carry

    def part_at(which):
        return pl.ds(pl.multiple_of(which * part, part), part)

    def rz_copy(i):
        other = (zo + i) % owners
        return remote(
            qb.at[part_at(other)],
            rz.at[zo],
            rz_send.at[other],
            rz_recv.at[zo],
            at_tok(z_peer(i)),
        )

    def rz_arrival(i):
        other = (zo + i) % owners
        return remote(
            qb.at[part_at(other)],
            rz.at[other],
            rz_send.at[other],
            rz_recv.at[other],
            at_tok(z_peer(i)),
        )

    pad_at = local_heads * 96
    qb[pl.ds(pad_at, EIGHTH - pad_at)] = jnp.zeros((EIGHTH - pad_at, dim), jnp.bfloat16)
    order = far_first(owners)

    here = core * 4 + yl * 2

    def shared(lane, which, send, recv, index, dev):
        piece = wsum.at[lane, part_at(which)]
        return remote(piece, piece, send.at[index], recv.at[index], at_tok(dev))

    def az_copy(i):
        piece = wsum.at[here + zp, part_at(zo)]
        return remote(
            piece, piece, az_send.at[(zo + i) % owners], az_recv.at[zo], at_tok(z_peer(i))
        )

    def az_arrival(i):
        other = (zo + i) % owners
        return shared(here + zp, other, az_send, az_recv, other, z_peer(i))

    def ap_copy(lane_pair, which):
        return shared(here + lane_pair, which, ap_send, ap_recv, which, pair)

    def ay_copy(lane_y, lane_pair, which):
        lane = core * 4 + lane_y * 2 + lane_pair
        return shared(lane, which, ay_send, ay_recv, lane_pair * owners + which, y_peer)

    def ac_copy(lane_core, lane_y, lane_pair, which):
        lane = lane_core * 4 + lane_y * 2 + lane_pair
        index = (lane_y * 2 + lane_pair) * owners + which
        return shared(lane, which, ac_send, ac_recv, index, partner)

    def ring(i):
        return (zo + i) % owners

    def arrived(slot):
        wait_recv(k_copy[slot])
        wait_recv(v_copy[slot])

    lax.fori_loop(0, local_heads, core_stage, 0)
    tokens_in(0)
    tokens_out(1)
    lax.fori_loop(0, local_heads, queries, 0)
    absorb(k_ref, v_ref, 0, first=True)
    tokens_in(1)
    tokens_out(2)
    lax.fori_loop(0, local_heads, y_stage, 0)
    for slot in (1, 2):
        start(v_copy[slot], 1)
    for off in offsets:
        tot_copy(off).wait_recv()
    arrived(5)
    absorb_slot(5)
    lax.fori_loop(0, local_heads, pair_stage, 0)
    tokens_in(2)
    for i in order:
        rz_copy(i).start()

    for slot in (1, 2):
        wait_recv(k_copy[slot])
    for slot in (0, 3):
        start(k_copy[slot])
    for slot in (4, 6):
        start(k_copy[slot])
    for slot in (1, 2):
        wait_recv(v_copy[slot])
    for slot in (4, 6):
        start(v_copy[slot])
    absorb_slot(1)
    absorb_slot(2)
    arrived(4)
    absorb_slot(4)

    summed = qb[part_at(zo)].astype(jnp.float32)
    for i in order:
        rz_arrival(i).wait_recv()
        summed = summed + rz[ring(i)].astype(jnp.float32)
    wsum[here + zp, part_at(zo)] = summed.astype(jnp.bfloat16)
    for i in order:
        az_copy(i).start()
    ap_copy(zp, zo).start()
    ay_copy(yl, zp, zo).start()
    ac_copy(core, yl, zp, zo).start()
    for slot in (0, 3):
        start(v_copy[slot], 0)

    arrived(6)
    absorb_slot(6)

    for i in order:
        az_arrival(i).wait_recv()
        ap_copy(zp, ring(i)).start()
        ay_copy(yl, zp, ring(i)).start()
        ac_copy(core, yl, zp, ring(i)).start()
    for slot in (0, 3):
        start(v_copy[slot], 1)
    for i in [0] + order:
        ap_copy(1 - zp, ring(i)).wait_recv()
        ay_copy(yl, 1 - zp, ring(i)).start()
        ac_copy(core, yl, 1 - zp, ring(i)).start()
    for slot in (0, 3):
        wait_recv(k_copy[slot])
    start(k_copy[7])
    for slot in (0, 3):
        v_copy[slot][0].wait_recv()
    start(v_copy[7], 0)
    absorb_slot(0, 0)
    absorb_slot(3, 0)
    for lane_pair in (zp, 1 - zp):
        for i in [0] + order:
            ay_copy(1 - yl, lane_pair, ring(i)).wait_recv()
            ac_copy(core, 1 - yl, lane_pair, ring(i)).start()

    wait_recv(k_copy[7])
    v_copy[7][0].wait_recv()
    absorb_slot(7, 0)
    for slot in (0, 3):
        v_copy[slot][1].wait_recv()
    start(v_copy[7], 1)
    absorb_slot(0, 1)
    absorb_slot(3, 1)
    for lane_y in range(2):
        for lane_pair in range(2):
            for which in range(owners):
                ac_copy(1 - core, lane_y, lane_pair, which).wait_recv()

    def sums(h, first, size):
        pieces = []
        for piece in range(first // 32, (first + size) // 32):
            start = pl.multiple_of(h * 96 + (piece % 3) * 32, 32)
            pieces.append(wsum[piece // 3, pl.ds(start, 32)].astype(jnp.float32))
        return jnp.concatenate(pieces, axis=0)

    def renewed(h, base, first, size):
        base = base.astype(jnp.float32)
        updated = base - sums(h, first, size)
        norm = jnp.sqrt(jnp.sum(base * base, axis=0, keepdims=True))
        squares = jnp.sum(updated * updated, axis=0, keepdims=True)
        return (updated * (norm / jnp.sqrt(squares + epsilon))).astype(jnp.bfloat16)

    def apply_fast(h, carry):
        query_unit = qu[h]
        query_hidden = []
        for half in range(2):
            at = half * 128
            gate = dot(query_unit, renewed(h, fi_ref[h, :, at : at + 128], at, 128))
            lin = dot(
                query_unit,
                renewed(h, fi_ref[h, :, hid + at : hid + at + 128], 256 + at, 128),
            )
            query_hidden.append((silu_parts(gate)[1] * lin).astype(jnp.bfloat16))
        new_out = renewed(h, fo_ref[h], 512, hid)
        fast[h] = dot(jnp.concatenate(query_hidden, axis=1), new_out)
        return carry

    def finish(h, carry):
        attended = jnp.transpose(acc[h] / l_ref[pl.ds(h, 1)])
        out_ref[h] = (attended + fast[h]).astype(jnp.bfloat16)
        return carry

    def out_copy(h):
        return pltpu.make_async_copy(out_ref.at[h], out_hbm.at[h], out_sem.at[h])

    lax.fori_loop(0, local_heads, apply_fast, 0, unroll=True)
    v_copy[7][1].wait_recv()
    absorb_slot(7, 1)
    lax.fori_loop(0, local_heads, finish, 0, unroll=True)

    for i in range(1, n_head):
        ss_copy(i).wait_send()
    for off in offsets:
        tot_copy(off).wait_send()
    for slot in range(8):
        for copy in k_copy[slot] + v_copy[slot]:
            copy.wait_send()

    def sent(h, carry):
        rc_copy(h).wait_send()
        ry_copy(h).wait_send()
        rp_copy(h).wait_send()
        return carry

    lax.fori_loop(0, local_heads, sent, 0)
    for i in order:
        rz_copy(i).wait_send()
        az_copy(i).wait_send()
    for which in range(owners):
        ap_copy(zp, which).wait_send()
        for lane_pair in range(2):
            ay_copy(yl, lane_pair, which).wait_send()
            for lane_y in range(2):
                ac_copy(core, lane_y, lane_pair, which).wait_send()
    for h in range(local_heads):
        out_copy(h).start()
    for h in range(local_heads):
        out_copy(h).wait()


def body(q, k, v, q_gain, k_gain, rate_in, rate_out, fast_in, fast_out, half_window, boundaries):
    rows, heads, dim = q.shape
    n_tok = lax.axis_size("tok")
    n_head = lax.axis_size("head")
    owners = n_tok // 8
    part = EIGHTH // owners
    bf16 = jnp.bfloat16
    f32 = jnp.float32
    hbm = pl.BlockSpec(memory_space=pl.ANY)
    smem = pl.BlockSpec(memory_space=pltpu.SMEM)
    dma = pltpu.SemaphoreType.DMA

    def call(*refs):
        kernel(heads * n_head, n_tok, n_head, *refs)

    result = pl.pallas_call(
        call,
        out_shape=jax.ShapeDtypeStruct((heads, rows, dim), bf16),
        in_specs=[hbm] * 9 + [smem] * 2,
        out_specs=hbm,
        scratch_shapes=[
            pltpu.VMEM((heads, rows, dim), bf16),
            pltpu.VMEM((heads, rows, dim), bf16),
            pltpu.VMEM((heads, rows, dim), bf16),
            pltpu.VMEM((heads, dim), f32),
            pltpu.VMEM((heads, dim), f32),
            pltpu.VMEM((heads, rows), f32),
            pltpu.VMEM((heads, rows), f32),
            pltpu.VMEM((heads, dim, 512), bf16),
            pltpu.VMEM((heads, 256, dim), bf16),
            pltpu.VMEM((heads, rows, dim), bf16),
            dma((9,)),
            dma((heads,)),
            pltpu.VMEM((8, heads, rows, dim), bf16),
            pltpu.VMEM((8, heads, rows, dim), bf16),
            pltpu.VMEM((8, rows), f32),
            pltpu.VMEM((n_head, 8, rows), f32),
            pltpu.VMEM((9, 8, rows), f32),
            pltpu.VMEM((heads, dim, rows), bf16),
            pltpu.VMEM((heads, rows, dim), bf16),
            pltpu.VMEM((8, rows), f32),
            pltpu.VMEM((8, rows), f32),
            pltpu.VMEM((heads, dim, rows), f32),
            pltpu.VMEM((heads, rows, 512), f32),
            pltpu.VMEM((heads, rows, dim), bf16),
            pltpu.VMEM((heads, rows, 256), f32),
            pltpu.VMEM((heads, HEAD_ROWS, dim), bf16),
            pltpu.VMEM((heads, HEAD_ROWS // 2, dim), bf16),
            pltpu.VMEM((heads, HEAD_ROWS // 4, dim), bf16),
            pltpu.VMEM((heads, HEAD_ROWS // 4, dim), bf16),
            pltpu.VMEM((heads, HEAD_ROWS // 8, dim), bf16),
            pltpu.VMEM((heads, HEAD_ROWS // 8, dim), bf16),
            pltpu.VMEM((EIGHTH, dim), bf16),
            pltpu.VMEM((owners, part, dim), bf16),
            pltpu.VMEM((8, EIGHTH, dim), bf16),
            pltpu.VMEM((heads, rows, dim), f32),
            dma((n_head,)),
            dma((n_head,)),
            dma((9,)),
            dma((9,)),
            dma((16,)),
            dma((16,)),
            dma((16,)),
            dma((16,)),
            dma((heads,)),
            dma((heads,)),
            dma((heads,)),
            dma((heads,)),
            dma((heads,)),
            dma((heads,)),
            dma((owners,)),
            dma((owners,)),
            dma((owners,)),
            dma((owners,)),
            dma((owners,)),
            dma((owners,)),
            dma((2 * owners,)),
            dma((2 * owners,)),
            dma((4 * owners,)),
            dma((4 * owners,)),
            pltpu.SemaphoreType.REGULAR((6,)),
        ],
        compiler_params=pltpu.CompilerParams(
            collective_id=0, has_side_effects=True, vmem_limit_bytes=60 * 1024 * 1024
        ),
    )(
        jnp.transpose(q, (1, 0, 2)),
        jnp.transpose(k, (1, 0, 2)),
        jnp.transpose(v, (1, 0, 2)),
        q_gain,
        k_gain,
        rate_in,
        rate_out,
        fast_in,
        fast_out,
        half_window,
        boundaries,
    )
    return jnp.transpose(result, (1, 0, 2))


def solution(mesh):
    in_specs = (
        P("tok", "head", None),
        P("tok", "head", None),
        P("tok", "head", None),
        P("head", None),
        P("head", None),
        P("head", "tok"),
        P("head", "tok"),
        P("head", None, None),
        P("head", None, None),
        P("head"),
        P(),
    )
    out_specs = P("tok", "head", None)
    return jax.shard_map(body, mesh=mesh, in_specs=in_specs, out_specs=out_specs, check_vma=False)
```
